32 devices in a mesh: lat: 4 (over y, core), lon: 8 (over z, x).
Axes of the slice: x: 2, y: 2, z: 4, core: 2. Of those that a mesh axis runs over, the one named last changes fastest.
Arguments:
- inputs: bfloat16 [8, 24, 96, 192], P(None, 'lat', 'lon'), may hold values from -6 to 6
- cotangent: bfloat16 [8, 24, 96, 192], P(None, 'lat', 'lon'), may hold values from -6 to 6
- qkv_weight: bfloat16 [192, 576], P(None, 'lon'), may hold values from -0.4375 to 0.4375
- proj_weight: bfloat16 [192, 192], P(None, 'lon'), may hold values from -0.4375 to 0.4375
- up_weight: bfloat16 [192, 768], P(None, 'lon'), may hold values from -0.4375 to 0.4375
- down_weight: bfloat16 [768, 192], P(None, 'lon'), may hold values from -0.21875 to 0.21875
- norm_gains: bfloat16 [2, 192], P(None, 'lon'), may hold values from 0.099609375 to 1.8984375
- bias_table: bfloat16 [16, 6, 20736], P(None, None, 'lon'), may hold values from -4 to 304
- type_of: int32 [4, 4], replicated, may hold values from 0 to 15
- region: int32 [8, 24], P(None, 'lat'), may hold values from 0 to 2
Outputs:
- grad_input: bfloat16 [8, 24, 96, 192], P(None, 'lat', 'lon')
- grad_qkv: float32 [192, 576], P(None, 'lon')
- grad_proj: float32 [192, 192], P(None, 'lon')
- grad_up: float32 [192, 768], P(None, 'lon')
- grad_down: float32 [768, 192], P(None, 'lon')
- grad_gains: float32 [2, 192], P(None, 'lon')
- grad_table: float32 [16, 6, 20736], P(None, None, 'lon')
The draws below stay inside these ranges and needn't reach their ends.
Inputs may be any that keep to these rules, and one draw needn't show every extreme that they name: `type_of`: types may repeat and some may be absent. Attention joins only tokens of a window with equal region ids.
All inputs are finite; a program needn't handle non-finite values.
Results may differ from the reference program's by a relative error of at most 0.015.
Values may be sent and summed in bfloat16 or wider, within the bound.
A program may use at most 64 MiB of HBM per device.

```python
import math
import jax
import jax.numpy as jnp
from jax import lax

WPL = 2
WLAT = 6
WLON = 12
WIN = 144
D = 192
HEADS = 6
FFN = 768
PLW = 4
LATW_DEV = 1
PLEV = 8
LAT_ROWS = 24
LON_COLS = 96
TYPES = 16
TOKENS = 18432
N_LAT = 4


def draw_bias_table(key, part):
    key_base = jax.random.fold_in(key, 0)
    base_vals = jnp.clip(jax.random.normal(key_base, (TYPES, HEADS, WIN, WIN), jnp.float32), -4.0, 4.0)
    return base_vals.reshape(TYPES, HEADS, WIN * WIN).astype(jnp.bfloat16)


def with_ends(values, own_key, smallest, high):
    longest = values.shape.index(max(values.shape))
    spots = []
    for shift in (0, 1):
        where = [jax.random.randint(jax.random.fold_in(own_key, axis), (), 0, length) for axis, length in enumerate(values.shape)]
        where[longest] = (where[longest] + shift) % values.shape[longest]
        spots.append(tuple(where))
    return values.at[spots[0]].set(smallest).at[spots[1]].set(high)


def levels(stream_key, dims, shards, smallest, top_value):
    def one(position, blocks):
        draws = jax.random.uniform(jax.random.fold_in(jax.random.fold_in(stream_key, 6), position), (blocks,), jnp.float32, smallest / len(shards), top_value / len(shards))
        return jnp.repeat(jnp.exp(draws), dims[position] // blocks).reshape((-1,) + (1,) * (len(dims) - position - 1))

    level = one(*shards[0])
    for cut in shards[1:]:
        level = level * one(*cut)
    return level


def bell_draw(key, extent, width, bound, pieces=(), held_as=jnp.bfloat16):
    loudness = levels(key, extent, pieces, -0.22, 0.18) if pieces else 1.0
    entries = jax.random.normal(key, extent, jnp.float32) * width * loudness
    return jnp.minimum(jnp.maximum(entries, -bound), bound).astype(held_as)


def setup_inputs(seed: int = 0) -> dict:
    splits = jax.random.split(jax.random.key(seed), 11)
    return {
        "inputs": bell_draw(splits[0], (PLEV, LAT_ROWS, LON_COLS, D), 1.0, 6.0, ((1, 4), (2, 8))),
        "cotangent": bell_draw(splits[1], (PLEV, LAT_ROWS, LON_COLS, D), 1.0, 6.0, ((1, 4), (2, 8))),
        "qkv_weight": bell_draw(splits[2], (D, 3 * D), D ** -0.5, 0.4375, ((1, 8),)),
        "proj_weight": bell_draw(splits[3], (D, D), D ** -0.5, 0.4375, ((1, 8),)),
        "up_weight": bell_draw(splits[4], (D, FFN), D ** -0.5, 0.4375, ((1, 8),)),
        "down_weight": bell_draw(splits[5], (FFN, D), FFN ** -0.5, 0.21875, ((1, 8),)),
        "norm_gains": jnp.clip(1.0 + 0.18 * jax.random.normal(splits[6], (2, D), jnp.float32), 0.099609375, 1.8984375).astype(jnp.bfloat16),
        "bias_table": draw_bias_table(jax.random.fold_in(splits[10], 71), 0),
        "type_of": with_ends(jax.random.randint(splits[8], (PLW, LATW_DEV * N_LAT), 0, TYPES), jax.random.fold_in(splits[8], 1), 0, TYPES - 1).astype(jnp.int32),
        "region": with_ends(jax.random.randint(splits[9], (PLEV, LAT_ROWS), 0, 3), jax.random.fold_in(splits[9], 1), 0, 2).astype(jnp.int32),
    }


def layer_norm(values):
    row_mean = lax.optimization_barrier(jnp.mean(values, axis=-1, keepdims=True))
    centred = values - row_mean
    variance = lax.optimization_barrier(jnp.mean(centred * centred, axis=-1, keepdims=True))
    inv_std = lax.rsqrt(variance + 1e-05)
    return (centred * inv_std, inv_std)

def norm_back(d_normed, normed, inv_std):
    return inv_std * (d_normed - lax.optimization_barrier(jnp.mean(d_normed, axis=-1, keepdims=True)) - normed * lax.optimization_barrier(jnp.mean(d_normed * normed, axis=-1, keepdims=True)))

def gelu_pair(pre_act):
    cumul = 0.5 * (1.0 + lax.erf(pre_act * 0.7071067811865476))
    density = jnp.exp(-0.5 * pre_act * pre_act) * 0.3989422804014327
    return (pre_act * cumul, cumul + pre_act * density)

def to_windows(column, level_windows, row_windows):
    features = column.shape[-1]
    shaped = column.reshape(level_windows, WPL, row_windows, WLAT, WLON, features)
    return shaped.transpose(0, 2, 1, 3, 4, 5).reshape(level_windows * row_windows * WIN, features)

def from_windows(flat, level_windows, row_windows):
    features = flat.shape[-1]
    shaped = flat.reshape(level_windows, row_windows, WPL, WLAT, WLON, features)
    return shaped.transpose(0, 2, 1, 3, 4, 5).reshape(level_windows * WPL, row_windows * WLAT, WLON, features)

def region_mask(region_rows, level_windows, row_windows):
    labels = region_rows.reshape(level_windows, WPL, row_windows, WLAT).transpose(0, 2, 1, 3)
    labels = jnp.broadcast_to(labels[..., None], (level_windows, row_windows, WPL, WLAT, WLON))
    labels = labels.reshape(level_windows, row_windows, WIN)
    return labels[..., :, None] == labels[..., None, :]

def column_grads(column, cot_column, weights, bias_pos, same_region):
    qkv_full, proj_full, up_full, down_full, gains_full = weights
    f32 = jnp.float32
    bf16 = jnp.bfloat16
    level_windows = column.shape[0] // WPL
    row_windows = column.shape[1] // WLAT
    features = column.shape[-1]
    head_count = bias_pos.shape[2]
    head_size = features // head_count
    factor = 1.0 / math.sqrt(head_size)
    gain_one = gains_full[0].astype(f32)
    gain_two = gains_full[1].astype(f32)
    window_cells = to_windows(column, level_windows, row_windows).astype(f32)
    normed_one, inv_one = layer_norm(window_cells)
    scaled_one = (normed_one * gain_one).astype(bf16)
    packed = jnp.dot(scaled_one, qkv_full, preferred_element_type=f32).astype(bf16)
    packed = packed.reshape(level_windows, row_windows, WIN, 3, head_count, head_size)
    queries = packed[:, :, :, 0]
    key_rows = packed[:, :, :, 1]
    value_rows = packed[:, :, :, 2]
    scores = jnp.einsum('abthd,abshd->abhts', queries.astype(f32), key_rows.astype(f32)) * factor
    scores = scores + bias_pos.astype(f32)
    scores = jnp.where(same_region[:, :, None], scores, -jnp.inf)
    peak_score = lax.optimization_barrier(jnp.max(scores, axis=-1, keepdims=True))
    raised = jnp.exp(scores - peak_score)
    attn_probs = raised / lax.optimization_barrier(jnp.sum(raised, axis=-1, keepdims=True))
    probs_b = attn_probs.astype(bf16)
    attended = jnp.einsum('abhts,abshd->abthd', probs_b.astype(f32), value_rows.astype(f32))
    attended = attended.astype(bf16).reshape(-1, features)
    middle = window_cells + jnp.dot(attended, proj_full, preferred_element_type=f32)
    normed_two, inv_two = layer_norm(middle)
    scaled_two = (normed_two * gain_two).astype(bf16)
    pre_act = jnp.dot(scaled_two, up_full, preferred_element_type=f32)
    activated, gelu_slope = gelu_pair(pre_act)
    hidden_b = activated.astype(bf16)
    cot_rows = to_windows(cot_column, level_windows, row_windows)
    grad_down = jnp.dot(hidden_b.T, cot_rows, preferred_element_type=f32)
    d_hidden = (jnp.dot(cot_rows, down_full.T, preferred_element_type=f32) * gelu_slope).astype(bf16)
    grad_up = jnp.dot(scaled_two.T, d_hidden, preferred_element_type=f32)
    d_htwo = jnp.dot(d_hidden, up_full.T, preferred_element_type=f32)
    gain_grad_two = lax.optimization_barrier(jnp.sum(d_htwo * normed_two, axis=0))
    d_middle = cot_rows.astype(f32) + norm_back(d_htwo * gain_two, normed_two, inv_two)
    d_middle_b = d_middle.astype(bf16)
    grad_proj = jnp.dot(attended.T, d_middle_b, preferred_element_type=f32)
    d_att = jnp.dot(d_middle_b, proj_full.T, preferred_element_type=f32).astype(bf16)
    d_att = d_att.reshape(level_windows, row_windows, WIN, head_count, head_size)
    d_prob = jnp.einsum('abthd,abshd->abhts', d_att.astype(f32), value_rows.astype(f32))
    d_values = jnp.einsum('abhts,abthd->abshd', probs_b.astype(f32), d_att.astype(f32))
    d_score = attn_probs * (d_prob - lax.optimization_barrier(jnp.sum(attn_probs * d_prob, axis=-1, keepdims=True)))
    d_score_b = d_score.astype(bf16)
    d_queries = jnp.einsum('abhts,abshd->abthd', d_score_b.astype(f32), key_rows.astype(f32)) * factor
    d_keys = jnp.einsum('abhts,abthd->abshd', d_score_b.astype(f32), queries.astype(f32)) * factor
    d_packed = jnp.stack([d_queries, d_keys, d_values], axis=3).astype(bf16).reshape(-1, 3 * features)
    grad_qkv = jnp.dot(scaled_one.T, d_packed, preferred_element_type=f32)
    d_hone = jnp.dot(d_packed, qkv_full.T, preferred_element_type=f32)
    gain_grad_one = lax.optimization_barrier(jnp.sum(d_hone * normed_one, axis=0))
    d_cells = d_middle + norm_back(d_hone * gain_one, normed_one, inv_one)
    d_column = from_windows(d_cells.astype(bf16), level_windows, row_windows)
    param_grads = (grad_qkv, grad_proj, grad_up, grad_down, jnp.stack([gain_grad_one, gain_grad_two]))
    table_grad = d_score.reshape(level_windows * row_windows, head_count, WIN * WIN)
    return (d_column, param_grads, table_grad)

def reference(inputs, cotangent, qkv_weight, proj_weight, up_weight, down_weight, norm_gains, bias_table, type_of, region):
    shifts = (-(WPL // 2), -(WLAT // 2), -(WLON // 2))
    shifted = jnp.roll(inputs, shifts, (0, 1, 2))
    cot_shifted = jnp.roll(cotangent, shifts, (0, 1, 2))
    lat_windows = LATW_DEV * N_LAT
    lon_windows = LON_COLS // WLON
    features = inputs.shape[-1]
    head_count = bias_table.shape[1]
    bias_pos = bias_table[type_of].reshape(PLW, lat_windows, head_count, WIN, WIN)
    same_region = region_mask(region, PLW, lat_windows)
    columns = shifted.reshape(PLEV, LAT_ROWS, lon_windows, WLON, features).transpose(2, 0, 1, 3, 4)
    cot_columns = cot_shifted.reshape(PLEV, LAT_ROWS, lon_windows, WLON, features).transpose(2, 0, 1, 3, 4)
    weights = (qkv_weight, proj_weight, up_weight, down_weight, norm_gains)

    def advance(totals, column_pair):
        d_column, param_grads, table_grad = column_grads(column_pair[0], column_pair[1], weights, bias_pos, same_region)
        return (jax.tree.map(jnp.add, totals, (param_grads, table_grad)), d_column)
    initial = (tuple((jnp.zeros(member.shape, jnp.float32) for member in weights)), jnp.zeros((PLW * lat_windows, head_count, WIN * WIN), jnp.float32))
    totals, d_columns = lax.scan(advance, initial, (columns, cot_columns))
    d_shifted = d_columns.transpose(1, 2, 0, 3, 4).reshape(PLEV, LAT_ROWS, LON_COLS, features)
    grad_input = jnp.roll(d_shifted, (WPL // 2, WLAT // 2, WLON // 2), (0, 1, 2))
    factor = 1.0 / math.sqrt(TOKENS)
    param_grads, table_sum = totals
    onehot = (type_of.reshape(-1)[:, None] == jnp.arange(TYPES, dtype=jnp.int32)[None, :]).astype(jnp.float32)
    grad_table = jnp.dot(onehot.T, table_sum.reshape(PLW * lat_windows, -1), precision=lax.Precision.HIGHEST).reshape(TYPES, head_count, WIN * WIN)
    return (grad_input, param_grads[0] * factor, param_grads[1] * factor, param_grads[2] * factor, param_grads[3] * factor, param_grads[4] * factor, grad_table)
```

```python
import functools
import math

import jax
import jax.numpy as jnp
from jax import lax
from jax.experimental import pallas as pl
from jax.experimental.pallas import tpu as pltpu
from jax.sharding import PartitionSpec as P

WPL = 2
WLAT = 6
WLON = 12
WIN = 144
MESH = pl.DeviceIdType.MESH
F32 = jnp.float32
BF16 = jnp.bfloat16


def layer_norm(values):
    row_mean = jnp.mean(values, axis=-1, keepdims=True)
    centred = values - row_mean
    variance = jnp.mean(centred * centred, axis=-1, keepdims=True)
    inv_std = lax.rsqrt(variance + 1e-05)
    return (centred * inv_std, inv_std)


def norm_back(d_normed, normed, inv_std):
    return inv_std * (
        d_normed
        - jnp.mean(d_normed, axis=-1, keepdims=True)
        - normed * jnp.mean(d_normed * normed, axis=-1, keepdims=True)
    )


def gelu_pair(pre_act):
    cumul = 0.5 * (1.0 + lax.erf(pre_act * 0.7071067811865476))
    density = jnp.exp(-0.5 * pre_act * pre_act) * 0.3989422804014327
    return (pre_act * cumul, cumul + pre_act * density)


def position(nlat, nlon):
    lat, lon = lax.axis_index("lat"), lax.axis_index("lon")

    def at(dlat, dlon):
        return (lax.rem(lat + dlat + nlat, nlat), lax.rem(lon + dlon + nlon, nlon))

    core, side = lax.rem(lat, 2), lax.rem(lon, 2)
    twin = (lat + 1 - 2 * core, lon)
    across = (lat, lon + 1 - 2 * side)
    return lat, lon, at, core, twin, across


def greet(devices):
    barrier = pltpu.get_barrier_semaphore()
    for device in devices:
        pl.semaphore_signal(barrier, inc=1, device_id=device, device_id_type=MESH)
    pl.semaphore_wait(barrier, len(devices))


def peers(nlat, nlon, at, twin, across):
    steps = [(0, d) for d in range(2, nlon, 2)] + [(d, 0) for d in range(2, nlat, 2)]
    steps += [(1, 0), (-1, 0), (0, 1), (0, -1), (1, 1), (-1, -1)]
    return [twin, across] + [at(*step) for step in steps]


def send(src, dst, send_sem, recv_sem, device):
    copy = pltpu.make_async_remote_copy(
        src_ref=src, dst_ref=dst, send_sem=send_sem, recv_sem=recv_sem, device_id=device, device_id_type=MESH
    )
    copy.start()
    return copy


def gather_kernel(nlat, nlon, a, d, b, h_lat, h_lon, h_diag, a_all, d_all, b_all, r_lat, r_lon, r_diag,
                  zs, zr, xs, xr, ts, tr, hs, hr):
    lat, lon, at, core, twin, across = position(nlat, nlon)
    greet(peers(nlat, nlon, at, twin, across))
    reach = nlon // 2
    srcs = (a.at[core], d.at[core], b)

    def slots(owner):
        return (a_all.at[owner, core], d_all.at[owner, core], b_all.at[owner])

    far, near, shared, halo = {}, {}, [], []
    for k in range(1, reach):
        for i in range(3):
            far[i, k] = send(srcs[i], slots(lon)[i], zs.at[i, k], zr.at[i, k], at(0, 2 * k))
    for i in range(3):
        near[i, 0] = send(srcs[i], slots(lon)[i], xs.at[i, 0], xr.at[i, 0], across)
    for i, (src, dst, step) in enumerate(
        ((h_lat, r_lat, (-1, 0)), (h_lon, r_lon, (0, -1)), (h_diag, r_diag, (-1, -1)))
    ):
        halo.append(send(src, dst, hs.at[i], hr.at[i], at(*step)))
    a_all[lon] = a[...]
    d_all[lon] = d[...]
    b_all[lon] = b[...]
    for k in range(1, reach):
        owner = lax.rem(lon - 2 * k + nlon, nlon)
        for i in range(3):
            slot = slots(owner)[i]
            far[i, k].wait_recv()
            near[i, k] = send(slot, slot, xs.at[i, k], xr.at[i, k], across)
            if i < 2:
                shared.append(send(slot, slot, ts.at[i, k], tr.at[i, k], twin))
    for k in range(reach):
        owner = lax.rem(across[1] - 2 * k + nlon, nlon)
        for i in range(3):
            slot = slots(owner)[i]
            near[i, k].wait_recv()
            if i < 2:
                shared.append(send(slot, slot, ts.at[i, reach + k], tr.at[i, reach + k], twin))
    for copy in list(far.values()) + list(near.values()):
        copy.wait_send()
    for copy in halo + shared:
        copy.wait()


def reduce_kernel(nlat, nlon, scale, a, d, t, kron, h_lat, h_lon, h_diag, a_out, d_out, t_out, r_lat, r_lon, r_diag,
                  a_twin, d_twin, a_half, d_half, a_x, d_x, t_x, a_mid, d_mid, t_mid, a_z, d_z, t_z,
                  a_row, d_row, t_row, cs, cr, xs, xr, zs, zr, ls, lr, fs, fr, hs, hr):
    lat, lon, at, core, twin, across = position(nlat, nlon)
    greet(peers(nlat, nlon, at, twin, across))
    reach = nlon // 2
    near, far, rest = {}, {}, []
    order = list(range(1, reach)) + [0]
    pairs = [
        send(src.at[1 - core], dst, cs.at[i], cr.at[i], twin)
        for i, (src, dst) in enumerate(((a, a_twin), (d, d_twin)))
    ]

    def cross(i, src, dst):
        for k in order:
            owner = lax.rem(across[1] + 2 * k, nlon)
            near[i, k] = send(src.at[owner], dst.at[k], xs.at[i, k], xr.at[i, k], across)

    cross(2, t, t_x)
    for i, (src, dst, step) in enumerate(
        ((h_lat, r_lat, (1, 0)), (h_lon, r_lon, (0, 1)), (h_diag, r_diag, (1, 1)))
    ):
        rest.append(send(src, dst, hs.at[i], hr.at[i], at(*step)))
    for i, (own, got, half, dst) in enumerate(((a, a_twin, a_half, a_x), (d, d_twin, d_half, d_x))):
        pairs[i].wait()
        half[...] = (own[core].astype(F32) + got[...].astype(F32)).astype(BF16)
        cross(i, half, dst)
    streams = ((2, t, t_x, t_mid, t_z), (0, a_half, a_x, a_mid, a_z), (1, d_half, d_x, d_mid, d_z))
    for i, own, got, mid, dst in streams:
        for k in range(1, reach):
            owner = lax.rem(lon + 2 * k, nlon)
            near[i, k].wait_recv()
            mid[k] = (own[owner].astype(F32) + got[k].astype(F32)).astype(BF16)
            far[i, k] = send(mid.at[k], dst.at[k], zs.at[i, k], zr.at[i, k], at(0, 2 * k))
    rows = nlat // 2
    row = lax.div(lat, 2)

    def total_of(i, own, got, dst):
        near[i, 0].wait_recv()
        total = own[lon].astype(F32) + got[0].astype(F32)
        for k in range(1, reach):
            far[i, k].wait_recv()
            total = total + dst[k].astype(F32)
        return total.astype(BF16)

    t_row[lat] = total_of(2, t, t_x, t_z)
    rest.append(send(t_row.at[lat], t_row.at[lat], ls.at[2, 0], lr.at[2, 0], twin))
    t_far = [send(t_row.at[lat], t_row.at[lat], ls.at[2, j], lr.at[2, j], at(2 * j, 0)) for j in range(1, rows)]
    halves = []
    for i, own, got, dst, line in ((0, a_half, a_x, a_z, a_row), (1, d_half, d_x, d_z, d_row)):
        line[row] = total_of(i, own, got, dst)
        halves.append(
            [send(line.at[row], line.at[row], ls.at[i, j], lr.at[i, j], at(2 * j, 0)) for j in range(1, rows)]
        )
    for j in range(1, rows):
        slot = t_row.at[lax.rem(lat - 2 * j + nlat, nlat)]
        t_far[j - 1].wait_recv()
        rest.append(send(slot, slot, fs.at[2, j], fr.at[2, j], twin))
    for i, (line, out) in enumerate(((a_row, a_out), (d_row, d_out))):
        for copy in halves[i]:
            copy.wait_recv()
        total = line[0].astype(F32)
        for j in range(1, rows):
            total = total + line[j].astype(F32)
        out[core] = total * scale
        rest.append(send(out.at[core], out.at[core], fs.at[i, 0], fr.at[i, 0], twin))
    for copy in list(near.values()) + list(far.values()) + t_far + halves[0] + halves[1]:
        copy.wait_send()
    for copy in rest:
        copy.wait()
    total = jnp.zeros(t_out.shape, F32)
    for i in range(nlat):
        total = total + jnp.dot(kron[i], t_row[i], preferred_element_type=F32)
    t_out[...] = total


def comm_call(kernel, collective_id, outs, scratch, operands):
    vmem = pl.BlockSpec(memory_space=pltpu.VMEM)
    return pl.pallas_call(
        kernel,
        out_shape=[jax.ShapeDtypeStruct(*o) for o in outs],
        in_specs=[vmem] * len(operands),
        out_specs=[vmem] * len(outs),
        scratch_shapes=scratch,
        compiler_params=pltpu.CompilerParams(
            collective_id=collective_id, has_side_effects=True, vmem_limit_bytes=48 * 2**20
        ),
    )(*operands)


def to_windows(grid):
    p, l, c = grid.shape[:3]
    shaped = grid.reshape(p // WPL, WPL, l // WLAT, WLAT, c // WLON, WLON, grid.shape[-1])
    return shaped.transpose(4, 0, 2, 1, 3, 5, 6).reshape(-1, grid.shape[-1])


def from_windows(flat, p, l, c):
    shaped = flat.reshape(c // WLON, p // WPL, l // WLAT, WPL, WLAT, WLON, flat.shape[-1])
    return shaped.transpose(1, 3, 2, 4, 0, 5, 6).reshape(p, l, c, flat.shape[-1])


def by_t(x, w_t):
    return lax.dot_general(x, w_t, (((1,), (1,)), ((), ())), preferred_element_type=F32)


def outer(x, y):
    return lax.dot_general(x, y, (((0,), (0,)), ((), ())), preferred_element_type=F32)


def plain(x, y):
    return jnp.dot(x, y, preferred_element_type=F32)


def pick_kernel(types, table, out):
    positions = types.shape[0]
    rows = [table[types[i]].astype(F32) for i in range(positions)]
    out[...] = jnp.concatenate(rows, axis=0).astype(BF16)


def pick_rows(types, table):
    _, head_count, part = table.shape
    return pl.pallas_call(
        pick_kernel,
        out_shape=jax.ShapeDtypeStruct((types.shape[0] * head_count, part), BF16),
        in_specs=[pl.BlockSpec(memory_space=pltpu.SMEM), pl.BlockSpec(memory_space=pltpu.VMEM)],
        out_specs=pl.BlockSpec(memory_space=pltpu.VMEM),
    )(types, table)


def window_kernel(n_up, n_qkv, n_proj, cells, cots, a_all, d_all, bias, label_col, label_row,
                  d_cells, ga, gd, table,
                  probs_s, qkv_t, proj_t, up_t, down_t, gains, g_qkv, g_proj, g_up, g_down, g_gain):
    owners, height = a_all.shape[0], a_all.shape[2]

    def joined(half, start, count):
        rows = [a_all[j, half].astype(F32)[start : start + count] for j in range(owners)]
        return jnp.concatenate(rows, axis=0).astype(BF16)

    up_t[...] = joined(0, 0, n_up)
    qkv_t[...] = joined(1, 0, n_qkv)
    proj_t[...] = joined(1, n_qkv, n_proj)
    wide = d_all.shape[3]
    for i in range(2):
        rows = [d_all[j, i].astype(F32) for j in range(owners)]
        down_t[:, i * wide : (i + 1) * wide] = jnp.concatenate(rows, axis=0).astype(BF16)
    gain_sum = a_all[0, 0].astype(F32)[n_up : n_up + 2]
    for j in range(1, owners):
        gain_sum = gain_sum + a_all[j, 0].astype(F32)[n_up : n_up + 2]
    gains[...] = gain_sum
    positions, head_count = bias.shape[:2]
    windows, _, features = cells.shape
    head_size = features // head_count
    factor = 1.0 / math.sqrt(head_size)
    for total in (g_qkv, g_proj, g_up, g_down, g_gain):
        total[...] = jnp.zeros(total.shape, F32)
    if windows > positions:
        table[...] = jnp.zeros(table.shape, F32)

    def body(w, carry):
        p = lax.rem(w, positions)
        gain_one, gain_two = gains[0:1], gains[1:2]
        lane_head = lax.broadcasted_iota(jnp.int32, (1, features), 1) // head_size
        heads = [(lane_head == h).astype(BF16) for h in range(head_count)]
        normed_one, inv_one = layer_norm(cells[w].astype(F32))
        scaled_one = (normed_one * gain_one).astype(BF16)
        q, k, v = (
            by_t(scaled_one, qkv_t[i * features : (i + 1) * features]).astype(BF16) for i in range(3)
        )
        same = label_col[p] == label_row[p]
        attended = jnp.zeros((WIN, features), F32)
        for h, head in enumerate(heads):
            scores = by_t(q * head, k) * factor + bias[p, h].astype(F32)
            scores = jnp.where(same, scores, -jnp.inf)
            raised = jnp.exp(scores - jnp.max(scores, axis=-1, keepdims=True))
            probs = raised * (1.0 / jnp.sum(raised, axis=-1, keepdims=True))
            probs_s[h] = probs
            attended = attended + plain(probs.astype(BF16), v * head)
        attended = attended.astype(BF16)
        middle = cells[w].astype(F32) + by_t(attended, proj_t[...])
        normed_two, inv_two = layer_norm(middle)
        scaled_two = (normed_two * gain_two).astype(BF16)
        cot = cots[w]
        activated, slope = gelu_pair(by_t(scaled_two, up_t[...]))
        g_down[...] += outer(cot, activated.astype(BF16))
        d_hidden = (plain(cot, down_t[...]) * slope).astype(BF16)
        g_up[...] += outer(d_hidden, scaled_two)
        d_htwo = plain(d_hidden, up_t[...])
        g_gain[1:2] += jnp.sum(d_htwo * normed_two, axis=0, keepdims=True)
        d_middle = cot.astype(F32) + norm_back(d_htwo * gain_two, normed_two, inv_two)
        d_middle_b = d_middle.astype(BF16)
        g_proj[...] += outer(d_middle_b, attended)
        d_att = plain(d_middle_b, proj_t[...]).astype(BF16)
        d_q, d_k, d_v = (jnp.zeros((WIN, features), F32) for _ in range(3))
        for h, head in enumerate(heads):
            probs, d_att_h = probs_s[h], d_att * head
            d_prob = by_t(d_att_h, v)
            d_v = d_v + outer(probs.astype(BF16), d_att_h)
            d_score = probs * (d_prob - jnp.sum(probs * d_prob, axis=-1, keepdims=True))
            if windows > positions:
                table[p, h] += d_score
            else:
                table[p, h] = d_score.astype(table.dtype)
            d_score_b = d_score.astype(BF16)
            d_q = d_q + plain(d_score_b, k * head)
            d_k = d_k + outer(d_score_b, q * head)
        d_hone = jnp.zeros((WIN, features), F32)
        for i, part in enumerate((d_q * factor, d_k * factor, d_v)):
            part = part.astype(BF16)
            span = slice(i * features, (i + 1) * features)
            g_qkv[span] += outer(part, scaled_one)
            d_hone = d_hone + plain(part, qkv_t[span])
        g_gain[0:1] += jnp.sum(d_hone * normed_one, axis=0, keepdims=True)
        d_cells[w] = (d_middle + norm_back(d_hone * gain_one, normed_one, inv_one)).astype(BF16)
        return carry

    lax.fori_loop(0, windows, body, 0)
    features = cells.shape[2]
    down = d_all.shape[2]
    gain_rows = jnp.concatenate([g_gain[...], jnp.zeros((height - n_up - 2, features), F32)], axis=0)
    spare = height - n_qkv - n_proj
    for j in range(owners):
        ga[0, j] = jnp.concatenate([g_up[j * n_up : (j + 1) * n_up], gain_rows], axis=0).astype(BF16)
        rows = [g_qkv[j * n_qkv : (j + 1) * n_qkv], g_proj[j * n_proj : (j + 1) * n_proj]]
        rows += [jnp.zeros((spare, features), F32)] if spare else []
        ga[1, j] = jnp.concatenate(rows, axis=0).astype(BF16)
        for i in range(2):
            gd[i, j] = g_down[j * down : (j + 1) * down, i * wide : (i + 1) * wide].astype(BF16)


def block_grads(cells, cots, a_all, d_all, cuts, bias, labels):
    features = cells.shape[1]
    positions, head_count = bias.shape[:2]
    windows, owners, wide = cells.shape[0] // WIN, a_all.shape[0], d_all.shape[3] * 2
    vmem = pl.BlockSpec(memory_space=pltpu.VMEM)
    outs = [((windows, WIN, features), BF16)]
    outs += [((2, owners) + x.shape[2:], BF16) for x in (a_all, d_all)]
    outs += [(bias.shape, F32 if windows > positions else BF16)]
    n_up, n_qkv, n_proj = cuts
    sizes = [(owners * n, features) for n in (n_qkv, n_proj, n_up)] + [(features, wide)]
    d_cells, *grads = pl.pallas_call(
        functools.partial(window_kernel, *cuts),
        out_shape=[jax.ShapeDtypeStruct(*o) for o in outs],
        in_specs=[vmem] * 7,
        out_specs=[vmem] * len(outs),
        scratch_shapes=[pltpu.VMEM((head_count, WIN, WIN), F32)]
        + [pltpu.VMEM(size, BF16) for size in sizes] + [pltpu.VMEM((2, features), F32)]
        + [pltpu.VMEM(size, F32) for size in sizes] + [pltpu.VMEM((2, features), F32)],
        compiler_params=pltpu.CompilerParams(vmem_limit_bytes=48 * 2**20),
    )(
        cells.reshape(windows, WIN, features), cots.reshape(windows, WIN, features),
        a_all, d_all, bias, labels[:, :, None], labels[:, None, :],
    )
    return (d_cells.reshape(cells.shape), *grads)


def shards_plain(inputs, cotangent, qkv_weight, proj_weight, up_weight, down_weight, norm_gains, bias_table, type_of, region):
    levels, rows, cols, features = inputs.shape
    nlat, nlon = lax.axis_size("lat"), lax.axis_size("lon")
    level_windows, row_windows = levels // WPL, rows // WLAT
    type_count, head_count, part = bias_table.shape
    positions = level_windows * row_windows
    lat_index = lax.axis_index("lat")
    row_half, col_half, level_shift = WLAT // 2, WLON // 2, WPL // 2
    all_types = type_of.reshape(level_windows, nlat, row_windows).transpose(1, 0, 2).reshape(nlat, positions)
    types = lax.dynamic_index_in_dim(all_types, lat_index, 0, keepdims=False)
    n_up, n_qkv, n_proj = up_weight.shape[1], qkv_weight.shape[1], proj_weight.shape[1]
    gain_cols, height = norm_gains.shape[1], -(-max(n_up + 2, n_qkv + n_proj) // 8) * 8
    gain_spot = lax.axis_index("lon") * gain_cols
    own_lane = jnp.arange(features, dtype=jnp.int32) // gain_cols == lax.axis_index("lon")
    gain_rows = jnp.where(own_lane, jnp.tile(norm_gains, (1, nlon)), jnp.zeros((), BF16))
    gain_rows = jnp.pad(gain_rows, ((0, height - n_up - 2), (0, 0)))
    a_part = jnp.stack(
        [
            jnp.concatenate([up_weight.T, gain_rows]),
            jnp.pad(
                jnp.concatenate([qkv_weight.T, proj_weight.T]), ((0, height - n_qkv - n_proj), (0, 0))
            ),
        ]
    )
    d_part = down_weight.reshape(2, -1, down_weight.shape[1]).transpose(0, 2, 1)
    b_part = pick_rows(types, bias_table)
    both = jnp.roll(jnp.stack([inputs, cotangent]), -level_shift, axis=1)
    rim_lat = both[:, :, :row_half, col_half:]
    rim_lon = both[:, :, row_half:, :col_half]
    rim_diag = both[:, :, :row_half, :col_half]
    flat = [r.reshape(-1, features) for r in (rim_lat, rim_lon, rim_diag)]
    dma = pltpu.SemaphoreType.DMA
    a_all, d_all, b_all, r_lat, r_lon, r_diag = comm_call(
        functools.partial(gather_kernel, nlat, nlon),
        0,
        [((nlon,) + x.shape, BF16) for x in (a_part, d_part, b_part)] + [(x.shape, BF16) for x in flat],
        [dma((3, nlon // 2))] * 4 + [dma((2, nlon))] * 2 + [dma((3,))] * 2,
        (a_part, d_part, b_part, *flat),
    )
    bias = b_all.transpose(1, 0, 2).reshape(positions, head_count, WIN, WIN)
    top = jnp.concatenate([both[:, :, row_half:, col_half:], r_lon.reshape(rim_lon.shape)], axis=3)
    bottom = jnp.concatenate([r_lat.reshape(rim_lat.shape), r_diag.reshape(rim_diag.shape)], axis=3)
    shifted = jnp.concatenate([top, bottom], axis=2)
    labels = region.reshape(level_windows, WPL, row_windows, WLAT).transpose(0, 2, 1, 3)
    labels = jnp.broadcast_to(labels[..., None], labels.shape + (WLON,)).reshape(positions, WIN)
    d_cells, ga, gd, table = block_grads(
        to_windows(shifted[0]), to_windows(shifted[1]), a_all, d_all, (n_up, n_qkv, n_proj), bias, labels
    )
    gt = table.astype(BF16).reshape(positions * head_count, nlon, part).transpose(1, 0, 2)
    onehot = (all_types[:, None, :] == jnp.arange(type_count, dtype=jnp.int32)[None, :, None]).astype(BF16)
    kron = jnp.einsum("lyp,gh->lygph", onehot, jnp.eye(head_count, dtype=BF16)).reshape(
        nlat, type_count * head_count, positions * head_count
    )
    back = from_windows(d_cells, levels, rows, cols)
    out_lat = back[:, rows - row_half :, : cols - col_half]
    out_lon = back[:, : rows - row_half, cols - col_half :]
    out_diag = back[:, rows - row_half :, cols - col_half :]
    flat = [r.reshape(-1, features) for r in (out_lat, out_lon, out_diag)]
    shard_shapes = (ga.shape[2:], gd.shape[2:], gt.shape[1:])
    token_count = levels * rows * cols * nlat * nlon
    a_sum, d_sum, t_sum, r_lat, r_lon, r_diag = comm_call(
        functools.partial(reduce_kernel, nlat, nlon, 1.0 / math.sqrt(token_count)),
        1,
        [((2,) + ga.shape[2:], F32), ((2,) + gd.shape[2:], F32), ((type_count * head_count, part), F32)]
        + [(x.shape, BF16) for x in flat],
        [pltpu.VMEM(x.shape[1:], BF16) for x in (ga, gd)] * 2
        + [pltpu.VMEM((nlon // 2,) + shape, BF16) for shape in shard_shapes] * 3
        + [pltpu.VMEM((nlat // 2,) + shape, BF16) for shape in shard_shapes[:2]]
        + [pltpu.VMEM((nlat,) + shard_shapes[2], BF16)]
        + [dma((2,))] * 2 + [dma((3, nlon // 2))] * 4 + [dma((3, nlat // 2))] * 4 + [dma((3,))] * 2,
        (ga, gd, gt, kron, *flat),
    )
    own = back[:, : rows - row_half, : cols - col_half]
    top = jnp.concatenate([r_diag.reshape(out_diag.shape), r_lat.reshape(out_lat.shape)], axis=2)
    bottom = jnp.concatenate([r_lon.reshape(out_lon.shape), own], axis=2)
    grad_input = jnp.roll(jnp.concatenate([top, bottom], axis=1), level_shift, axis=0)
    return (
        grad_input,
        a_sum[1, :n_qkv].T,
        a_sum[1, n_qkv : n_qkv + n_proj].T,
        a_sum[0, :n_up].T,
        d_sum.transpose(0, 2, 1).reshape(down_weight.shape),
        lax.dynamic_slice(a_sum[0, n_up : n_up + 2], (jnp.int32(0), gain_spot), (2, gain_cols)),
        t_sum.reshape(type_count, head_count, part),
    )


LANES = 128
SUB = 8


def rc(src, dst, send_sem, recv_sem, device):
    return pltpu.make_async_remote_copy(
        src_ref=src, dst_ref=dst, send_sem=send_sem, recv_sem=recv_sem, device_id=device, device_id_type=MESH
    )


def fused_kernel(nlat, nlon, cuts, scale, x_in, c_in, a, d, tab, types, label_q, label_k,
                 out, qkv_o, proj_o, up_o, down_o, gain_o, t_out,
                 grid, a_all, d_all, b_all,
                 wide_s, cells_s, cots_s, dcell_s, perm_s, asm_s, score_s, prob_b, ds_b, kexp_s, vexp_s,
                 pick_m, pick_t, pick_u,
                 qkv_t, proj_t, up_t, down_t, gains, g_qkv, g_proj, g_up, g_down, g_gain,
                 ga, gd, obuf, a_twin, d_twin, a_half, d_half, a_x, d_x, a_mid, d_mid, a_z, d_z, a_row, d_row,
                 a_fin, d_fin, t_w, t_x, t_mid, t_z, t_row, t_val,
                 own_s, hs, hr, wzs, wzr, wxs, wxr, wts, wtr, bzs, bzr, bxs, bxr,
                 txs, txr, tzs, tzr, tls, tlr, tfs, tfr,
                 pcs, pcr, pxs, pxr, pzs, pzr, pls, plr, pfs, pfr, ohs, ohr):
    n_up, n_qkv, n_proj = cuts
    lat, lon, at, core, twin, across = position(nlat, nlon)
    rows_c, cols_c, levels, features = x_in.shape
    half_r, half_c = rows_c // 2, cols_c // 2
    head_count = tab.shape[0]
    type_count = tab.shape[1]
    positions = label_q.shape[0]
    owners, height, wide = nlon, a.shape[1], d.shape[2]
    reach, rows_n = nlon // 2, nlat // 2
    head_size = features // head_count
    per = WIN // owners
    spare = WIN - LANES
    factor = 1.0 / math.sqrt(head_size)
    slab = WIN // WPL

    greet(peers(nlat, nlon, at, twin, across))

    tiles = [(t, t * LANES, min(LANES, features - t * LANES)) for t in range(-(-features // LANES))]

    def fill(ref, value):
        for t, start, count in tiles:
            ref[t, :, :count] = value[:, start : start + count]

    def whole(ref):
        return jnp.concatenate([ref[t][:, :count] for t, _, count in tiles], axis=1)

    def strided(ref, start, size, stride):
        return jnp.concatenate(
            [ref.at[t][pl.ds(start, size, stride=stride), :][:, :count] for t, _, count in tiles], axis=1
        )

    def store_strided(ref, start, size, stride, value):
        for t, first, count in tiles:
            piece = value[:, first : first + count]
            if count < LANES:
                piece = jnp.concatenate([piece, jnp.zeros((size, LANES - count), F32)], axis=1)
            ref.at[t][pl.ds(start, size, stride=stride), :] = piece

    def w_slots(owner):
        return (a_all.at[owner, core], d_all.at[owner, core])

    w_src = (a.at[core], d.at[core])

    def far_w(i, k):
        return rc(w_src[i], w_slots(lon)[i], wzs.at[i, k], wzr.at[i, k], at(0, 2 * k))

    for i in (0, 1):
        for k in range(1, reach):
            far_w(i, k).start()
        rc(w_src[i], w_slots(lon)[i], wxs.at[i, 0], wxr.at[i, 0], across).start()
    lo_r, hi_r = pl.ds(0, half_r), pl.ds(half_r, rows_c - half_r)
    lo_c, hi_c = pl.ds(0, half_c), pl.ds(half_c, cols_c - half_c)
    end_r, end_c = pl.ds(rows_c - half_r, half_r), pl.ds(cols_c - half_c, half_c)
    first_r, first_c = pl.ds(0, rows_c - half_r), pl.ds(0, cols_c - half_c)

    def halo(g, i):
        src = (x_in, c_in)[g]
        dst = grid.at[g]
        if i == 0:
            return rc(src.at[lo_r, hi_c], dst.at[end_r, first_c], hs.at[g, i], hr.at[g, i], at(-1, 0))
        if i == 1:
            return rc(src.at[hi_r, lo_c], dst.at[first_r, end_c], hs.at[g, i], hr.at[g, i], at(0, -1))
        return rc(src.at[lo_r, lo_c], dst.at[end_r, end_c], hs.at[g, i], hr.at[g, i], at(-1, -1))

    def own(g):
        return pltpu.make_async_copy((x_in, c_in)[g].at[hi_r, hi_c], grid.at[g].at[first_r, first_c], own_s.at[g])

    for g in (0, 1):
        own(g).start()
        for i in range(3):
            halo(g, i).start()

    rows_i = lax.broadcasted_iota(jnp.int32, (SUB, type_count), 0)
    want = jnp.full((SUB, type_count), -1, jnp.int32)
    for i in range(positions):
        want = jnp.where(rows_i == i, types[i, lat], want)
    onehot = (lax.broadcasted_iota(jnp.int32, (SUB, type_count), 1) == want).astype(F32).astype(BF16)
    tails = [jnp.zeros((per, LANES), F32) for _ in range(positions)]
    for h in range(head_count):
        val = jnp.dot(onehot, tab[h], preferred_element_type=F32)
        for r in range(per):
            pick_m[r * SUB : (r + 1) * SUB] = val[:, r * WIN : r * WIN + LANES]
            end = val[:, r * WIN + LANES : (r + 1) * WIN]
            pick_t[r * SUB : (r + 1) * SUB] = jnp.concatenate([end, jnp.zeros((SUB, LANES - spare), F32)], axis=1)
        for i in range(positions):
            pick_u[i, pl.ds(h, per, stride=SUB), :] = pick_m[pl.ds(i, per, stride=SUB), :]
            piece = pick_t[pl.ds(i, per, stride=SUB), :]
            tails[i] = tails[i] + (pltpu.roll(piece, h * spare, 1) if h else piece)
    for i in range(positions):
        pick_u[i, pl.ds(head_count, per, stride=SUB), :] = tails[i]
        for h in range(head_count + 1, SUB):
            pick_u[i, pl.ds(h, per, stride=SUB), :] = jnp.zeros((per, LANES), F32)

    def far_b(p, k):
        return rc(b_all.at[p, lon], b_all.at[p, lon], bzs.at[p, k], bzr.at[p, k], at(0, 2 * k))

    def relay_b(p):
        rc(b_all.at[p, lon], b_all.at[p, lon], bxs.at[p, 0], bxr.at[p, 0], across).start()
        for k in range(1, reach):
            far_b(p, k).wait_recv()
            slot = b_all.at[p, lax.rem(lon - 2 * k + nlon, nlon)]
            rc(slot, slot, bxs.at[p, k], bxr.at[p, k], across).start()

    def near_b(p, k):
        slot = b_all.at[p, lon]
        return rc(slot, slot, bxs.at[p, k], bxr.at[p, k], across)

    for i in range(positions):
        b_all[i, lon] = pick_u[i].astype(BF16)
    for i in range(positions):
        for k in range(1, reach):
            far_b(i, k).start()

    a_all[lon] = a[...]
    d_all[lon] = d[...]
    shared = []
    for k in range(1, reach):
        owner = lax.rem(lon - 2 * k + nlon, nlon)
        for i in (0, 1):
            slot = w_slots(owner)[i]
            far_w(i, k).wait_recv()
            rc(slot, slot, wxs.at[i, k], wxr.at[i, k], across).start()
            copy = rc(slot, slot, wts.at[i, k], wtr.at[i, k], twin)
            copy.start()
            shared.append(copy)
    relay_b(0)
    for g, store in ((0, cells_s), (1, cots_s)):
        own(g).wait()
        for i in range(3):
            halo(g, i).wait_recv()
        fill(wide_s, grid[g].astype(F32).reshape(rows_c * cols_c * levels, features))
        for i in range(positions):
            for j in range(WPL):
                level = (WPL * i + j + WPL // 2) % levels
                store[i, j * slab : (j + 1) * slab] = strided(wide_s, level, slab, levels)
    for k in range(reach):
        owner = lax.rem(across[1] - 2 * k + nlon, nlon)
        for i in (0, 1):
            slot = w_slots(owner)[i]
            rc(slot, slot, wxs.at[i, k], wxr.at[i, k], across).wait_recv()
            copy = rc(slot, slot, wts.at[i, reach + k], wtr.at[i, reach + k], twin)
            copy.start()
            shared.append(copy)
    for total in (g_qkv, g_proj, g_up, g_down, g_gain):
        total[...] = jnp.zeros(total.shape, F32)
    asm_s[...] = jnp.zeros(asm_s.shape, F32)
    for copy in shared:
        copy.wait_recv()

    def joined(half, start, count):
        rows = [a_all[j, half].astype(F32)[start : start + count] for j in range(owners)]
        return jnp.concatenate(rows, axis=0).astype(BF16)

    up_t[...] = joined(0, 0, n_up)
    qkv_t[...] = joined(1, 0, n_qkv)
    proj_t[...] = joined(1, n_qkv, n_proj)
    for i in range(2):
        rows = [d_all[j, i].astype(F32) for j in range(owners)]
        down_t[:, i * wide : (i + 1) * wide] = jnp.concatenate(rows, axis=0).astype(BF16)
    gain_sum = a_all[0, 0].astype(F32)[n_up : n_up + 2]
    for j in range(1, owners):
        gain_sum = gain_sum + a_all[j, 0].astype(F32)[n_up : n_up + 2]
    gains[...] = gain_sum

    def near_t(p, k):
        owner = lax.rem(across[1] + 2 * k, nlon)
        return rc(t_w.at[p, owner], t_x.at[p, k], txs.at[p, k], txr.at[p, k], across)

    def far_t(p, k):
        return rc(t_mid.at[p, k], t_z.at[p, k], tzs.at[p, k], tzr.at[p, k], at(0, 2 * k))

    order = list(range(1, reach)) + [0]

    def stage_one(p):
        for k in order:
            near_t(p, k).start()

    def stage_two(p):
        for k in range(1, reach):
            owner = lax.rem(lon + 2 * k, nlon)
            near_t(p, k).wait_recv()
            t_mid[p, k] = (t_w[p, owner].astype(F32) + t_x[p, k].astype(F32)).astype(BF16)
            far_t(p, k).start()

    def row_t(p, j):
        slot = t_row.at[lat, p]
        return rc(slot, slot, tls.at[p, j], tlr.at[p, j], at(2 * j, 0) if j else twin)

    def stage_three(p):
        near_t(p, 0).wait_recv()
        total = t_w[p, lon].astype(F32) + t_x[p, 0].astype(F32)
        for k in range(1, reach):
            far_t(p, k).wait_recv()
            total = total + t_z[p, k].astype(F32)
        t_row[lat, p] = total.astype(BF16)
        for j in list(range(1, rows_n)) + [0]:
            row_t(p, j).start()

    def fold_t(p, j):
        slot = t_row.at[lax.rem(lat - 2 * j + nlat, nlat), p]
        return rc(slot, slot, tfs.at[p, j], tfr.at[p, j], twin)

    def stage_four(p):
        for j in range(1, rows_n):
            row_t(p, j).wait_recv()
            fold_t(p, j).start()

    lane_head = lax.broadcasted_iota(jnp.int32, (1, features), 1) // head_size
    seg = lax.broadcasted_iota(jnp.int32, (1, LANES), 1) // spare

    def to_perm(value):
        fill(perm_s, value)
        return jnp.concatenate([strided(perm_s, r, SUB, per) for r in range(per)], axis=0)

    def from_perm(value):
        for r in range(per):
            store_strided(perm_s, r, SUB, per, value[r * SUB : (r + 1) * SUB])
        return whole(perm_s)

    def expand(dst, rows):
        low = rows[:LANES]
        high = rows[LANES:]
        ends = []
        for h in range(head_count):
            mine = lane_head == h
            dst[h * LANES : (h + 1) * LANES] = jnp.where(mine, low, 0.0).astype(BF16)
            ends.append(jnp.where(mine, high, 0.0))
        ends.append(jnp.zeros((LANES - head_count * spare, features), F32))
        dst[head_count * LANES :] = jnp.concatenate(ends, axis=0).astype(BF16)

    def collapse(big):
        low = big[:LANES]
        start = head_count * LANES
        high = big[start : start + spare]
        for h in range(1, head_count):
            mine = lane_head == h
            low = jnp.where(mine, big[h * LANES : (h + 1) * LANES], low)
            high = jnp.where(mine, big[start + h * spare : start + (h + 1) * spare], high)
        return jnp.concatenate([low, high], axis=0)

    def block(h):
        return slice(h * LANES, (h + 1) * LANES)

    def body(p, carry):
        gain_one, gain_two = gains[0:1], gains[1:2]
        normed_one, inv_one = layer_norm(cells_s[p])
        scaled_one = (normed_one * gain_one).astype(BF16)
        q, k, v = (by_t(scaled_one, qkv_t[i * features : (i + 1) * features]) for i in range(3))
        qp = to_perm(q).astype(BF16)
        expand(kexp_s, k)
        expand(vexp_s, v)
        for j in range(reach):
            near_b(p, j).wait_recv()
        for j in range(owners):
            asm_s[j * WIN : (j + 1) * WIN] = b_all[p, j].astype(F32)
        same = label_q[p] == label_k[p, 0:1]
        same_end = label_q[p] == label_k[p, 1:2]

        def bias_of(h):
            return jnp.concatenate([asm_s[pl.ds(r * SUB + h, SUB, stride=WIN), :] for r in range(per)], axis=0)

        def raw(h, keep):
            scores = by_t(qp, kexp_s[block(h)]) * factor + bias_of(h)
            return jnp.where(keep, scores, -jnp.inf)

        last = head_count
        s_end = raw(last, same_end)
        peak_end = jnp.zeros((WIN, LANES), F32)
        for h in range(head_count):
            mine = seg == h
            s = raw(h, same)
            peak = jnp.max(jnp.maximum(s, jnp.where(mine, s_end, -jnp.inf)), axis=-1, keepdims=True)
            score_s[h] = jnp.exp(s - peak)
            peak_end = jnp.where(mine, peak, peak_end)
        e_end = jnp.exp(s_end - peak_end)
        inv_end = jnp.zeros((WIN, LANES), F32)
        for h in range(head_count):
            mine = seg == h
            e = score_s[h]
            inv = 1.0 / jnp.sum(e + jnp.where(mine, e_end, 0.0), axis=-1, keepdims=True)
            probs = e * inv
            score_s[h] = probs
            prob_b[:, block(h)] = probs.astype(BF16)
            inv_end = jnp.where(mine, inv, inv_end)
        p_end = e_end * inv_end
        score_s[last] = p_end
        prob_b[:, block(last)] = p_end.astype(BF16)
        attended = from_perm(plain(prob_b[...], vexp_s[...])).astype(BF16)

        @pl.when(p + 1 < positions)
        def _():
            relay_b(p + 1)

        middle = cells_s[p] + by_t(attended, proj_t[...])
        normed_two, inv_two = layer_norm(middle)
        scaled_two = (normed_two * gain_two).astype(BF16)
        cot = cots_s[p].astype(BF16)
        activated, slope = gelu_pair(by_t(scaled_two, up_t[...]))
        g_down[...] += outer(cot, activated.astype(BF16))
        d_hidden = (plain(cot, down_t[...]) * slope).astype(BF16)
        g_up[...] += outer(d_hidden, scaled_two)
        d_htwo = plain(d_hidden, up_t[...])
        g_gain[1:2] += jnp.sum(d_htwo * normed_two, axis=0, keepdims=True)
        d_middle = cots_s[p] + norm_back(d_htwo * gain_two, normed_two, inv_two)
        d_middle_b = d_middle.astype(BF16)
        g_proj[...] += outer(d_middle_b, attended)
        dap = to_perm(plain(d_middle_b, proj_t[...])).astype(BF16)

        p_end = score_s[last]
        dp_end = by_t(dap, vexp_s[block(last)])
        mix_end = p_end * dp_end
        dot_end = jnp.zeros((WIN, LANES), F32)

        def put(h, ds):
            ds_b[:, block(h)] = ds.astype(BF16)
            for r in range(per):
                asm_s[pl.ds(r * SUB + h, SUB, stride=WIN), :] = ds[r * SUB : (r + 1) * SUB]

        for h in range(head_count):
            mine = seg == h
            probs = score_s[h]
            dp = by_t(dap, vexp_s[block(h)])
            dot = jnp.sum(probs * dp + jnp.where(mine, mix_end, 0.0), axis=-1, keepdims=True)
            dot_end = jnp.where(mine, dot, dot_end)
            put(h, probs * (dp - dot))
        put(last, p_end * (dp_end - dot_end))
        for j in range(owners):
            t_w[p, j] = asm_s[j * WIN : (j + 1) * WIN].astype(BF16)
        stage_one(p)
        d_q = from_perm(plain(ds_b[...], kexp_s[...]))
        d_k = collapse(outer(ds_b[...], qp))
        d_v = collapse(outer(prob_b[...], dap))
        d_hone = jnp.zeros((WIN, features), F32)
        for i, part in enumerate((d_q * factor, d_k * factor, d_v)):
            part = part.astype(BF16)
            span = slice(i * features, (i + 1) * features)
            g_qkv[span] += outer(part, scaled_one)
            d_hone = d_hone + plain(part, qkv_t[span])
        g_gain[0:1] += jnp.sum(d_hone * normed_one, axis=0, keepdims=True)
        dcell_s[p] = d_middle + norm_back(d_hone * gain_one, normed_one, inv_one)

        @pl.when(p >= 1)
        def _():
            stage_two(p - 1)

        @pl.when(p >= 2)
        def _():
            stage_three(p - 2)

        @pl.when(p >= 3)
        def _():
            stage_four(p - 3)

        return carry

    lax.fori_loop(0, positions, body, 0)

    down = d.shape[1]
    gain_rows = jnp.concatenate([g_gain[...], jnp.zeros((height - n_up - 2, features), F32)], axis=0)
    pad = height - n_qkv - n_proj
    for j in range(owners):
        ga[0, j] = jnp.concatenate([g_up[j * n_up : (j + 1) * n_up], gain_rows], axis=0).astype(BF16)
        rows = [g_qkv[j * n_qkv : (j + 1) * n_qkv], g_proj[j * n_proj : (j + 1) * n_proj]]
        rows += [jnp.zeros((pad, features), F32)] if pad else []
        ga[1, j] = jnp.concatenate(rows, axis=0).astype(BF16)
        for i in range(2):
            gd[i, j] = g_down[j * down : (j + 1) * down, i * wide : (i + 1) * wide].astype(BF16)
    pairs = [
        rc(src.at[1 - core], dst, pcs.at[i], pcr.at[i], twin)
        for i, (src, dst) in enumerate(((ga, a_twin), (gd, d_twin)))
    ]
    for copy in pairs:
        copy.start()
    for i in range(positions):
        for j in range(WPL):
            level = (WPL * i + j + WPL // 2) % levels
            store_strided(wide_s, level, slab, levels, dcell_s[i, j * slab : (j + 1) * slab])
    obuf[...] = whole(wide_s).reshape(obuf.shape).astype(BF16)
    outs = [
        rc(obuf.at[end_r, first_c], out.at[lo_r, hi_c], ohs.at[0], ohr.at[0], at(1, 0)),
        rc(obuf.at[first_r, end_c], out.at[hi_r, lo_c], ohs.at[1], ohr.at[1], at(0, 1)),
        rc(obuf.at[end_r, end_c], out.at[lo_r, lo_c], ohs.at[2], ohr.at[2], at(1, 1)),
    ]
    out[hi_r, hi_c] = obuf[first_r, first_c]
    halves = (a_half, d_half)
    p_x, p_mid, p_z = (a_x, d_x), (a_mid, d_mid), (a_z, d_z)

    def near_p(i, k):
        owner = lax.rem(across[1] + 2 * k, nlon)
        return rc(halves[i].at[owner], p_x[i].at[k], pxs.at[i, k], pxr.at[i, k], across)

    def far_p(i, k):
        return rc(p_mid[i].at[k], p_z[i].at[k], pzs.at[i, k], pzr.at[i, k], at(0, 2 * k))

    for i, (mine, got) in enumerate(((ga, a_twin), (gd, d_twin))):
        pairs[i].wait()
        halves[i][...] = (mine[core].astype(F32) + got[...].astype(F32)).astype(BF16)
        for k in order:
            near_p(i, k).start()
    for copy in outs:
        copy.start()
    for p in range(max(positions - 1, 0), positions):
        stage_two(p)
    for p in range(max(positions - 2, 0), positions - 1):
        stage_three(p)
    for p in range(max(positions - 3, 0), positions - 2):
        stage_four(p)
    for i in (0, 1):
        for k in range(1, reach):
            owner = lax.rem(lon + 2 * k, nlon)
            near_p(i, k).wait_recv()
            p_mid[i][k] = (halves[i][owner].astype(F32) + p_x[i][k].astype(F32)).astype(BF16)
            far_p(i, k).start()
    stage_three(positions - 1)
    for p in range(max(positions - 2, 0), positions - 1):
        stage_four(p)
    row = lax.div(lat, 2)
    lines, fins = (a_row, d_row), (a_fin, d_fin)

    def line_p(i, j):
        slot = lines[i].at[row]
        return rc(slot, slot, pls.at[i, j], plr.at[i, j], at(2 * j, 0))

    for i in (0, 1):
        near_p(i, 0).wait_recv()
        total = halves[i][lon].astype(F32) + p_x[i][0].astype(F32)
        for k in range(1, reach):
            far_p(i, k).wait_recv()
            total = total + p_z[i][k].astype(F32)
        lines[i][row] = total.astype(BF16)
        for j in range(1, rows_n):
            line_p(i, j).start()
    stage_four(positions - 1)

    def last_p(i):
        slot = fins[i].at[core]
        return rc(slot, slot, pfs.at[i], pfr.at[i], twin)

    for i in (0, 1):
        for j in range(1, rows_n):
            line_p(i, j).wait_recv()
        total = lines[i][0].astype(F32)
        for j in range(1, rows_n):
            total = total + lines[i][j].astype(F32)
        fins[i][core] = total * scale
        last_p(i).start()
    for p in range(positions):
        row_t(p, 0).wait_recv()
        for j in range(1, rows_n):
            fold_t(p, j).wait_recv()
    spots = nlat * positions
    for i in range(nlat):
        for p in range(positions):
            t_val[(i * positions + p) * WIN : (i * positions + p + 1) * WIN] = t_row[i, p].astype(F32)
    cols_i = lax.broadcasted_iota(jnp.int32, (type_count, spots), 1)
    want = jnp.full((type_count, spots), -1, jnp.int32)
    for i in range(nlat):
        for p in range(positions):
            want = jnp.where(cols_i == i * positions + p, types[p, i], want)
    by_type = (lax.broadcasted_iota(jnp.int32, (type_count, spots), 0) == want).astype(F32).astype(BF16)
    ends = [t_val[pl.ds(r * SUB + head_count, spots, stride=WIN), :] for r in range(per)]
    for h in range(head_count):
        pieces = []
        for r in range(per):
            pieces.append(t_val[pl.ds(r * SUB + h, spots, stride=WIN), :])
            pieces.append(ends[r][:, h * spare : (h + 1) * spare])
        flat = jnp.concatenate(pieces, axis=1).astype(BF16)
        t_out[h] = jnp.dot(by_type, flat, preferred_element_type=F32)
    for i in (0, 1):
        last_p(i).wait_recv()
    up_o[...] = a_fin[0][:n_up].T
    qkv_o[...] = a_fin[1][:n_qkv]
    proj_o[...] = a_fin[1][n_qkv : n_qkv + n_proj]
    for i in range(2):
        down_o[:, i * wide : (i + 1) * wide] = d_fin[i]
    gain_full = a_fin[0][n_up : n_up + 2]
    count = features // owners
    mine = gain_full[:, :count]
    for j in range(1, owners):
        mine = jnp.where(lon == j, gain_full[:, j * count : (j + 1) * count], mine)
    gain_o[...] = mine
    for copy in outs:
        copy.wait()
    for i in (0, 1):
        for k in range(1, reach):
            far_w(i, k).wait_send()
            far_p(i, k).wait_send()
        for k in range(reach):
            rc(w_slots(lon)[i], w_slots(lon)[i], wxs.at[i, k], wxr.at[i, k], across).wait_send()
            near_p(i, k).wait_send()
        for j in range(1, rows_n):
            line_p(i, j).wait_send()
        last_p(i).wait_send()
    for copy in shared:
        copy.wait_send()
    for g in (0, 1):
        for i in range(3):
            halo(g, i).wait_send()
    for p in range(positions):
        for k in range(reach):
            if k:
                far_b(p, k).wait_send()
                far_t(p, k).wait_send()
            near_b(p, k).wait_send()
            near_t(p, k).wait_send()
        for j in range(rows_n):
            row_t(p, j).wait_send()
            if j:
                fold_t(p, j).wait_send()


def shards_fused(inputs, cotangent, qkv_weight, proj_weight, up_weight, down_weight, norm_gains, bias_table, type_of, region):
    levels, rows, cols, features = inputs.shape
    nlat, nlon = lax.axis_size("lat"), lax.axis_size("lon")
    level_windows = levels // WPL
    type_count, head_count, part = bias_table.shape
    positions, owners, reach, rows_n = level_windows, nlon, nlon // 2, nlat // 2
    n_up, n_qkv, n_proj = up_weight.shape[1], qkv_weight.shape[1], proj_weight.shape[1]
    gain_cols, height = norm_gains.shape[1], -(-max(n_up + 2, n_qkv + n_proj) // 8) * 8
    own_lane = jnp.arange(features, dtype=jnp.int32) // gain_cols == lax.axis_index("lon")
    gain_rows = jnp.where(own_lane, jnp.tile(norm_gains, (1, nlon)), jnp.zeros((), BF16))
    gain_rows = jnp.pad(gain_rows, ((0, height - n_up - 2), (0, 0)))
    a_part = jnp.stack(
        [
            jnp.concatenate([up_weight.T, gain_rows]),
            jnp.pad(
                jnp.concatenate([qkv_weight.T, proj_weight.T]), ((0, height - n_qkv - n_proj), (0, 0))
            ),
        ]
    )
    d_part = down_weight.reshape(2, -1, down_weight.shape[1]).transpose(0, 2, 1)
    labels = region.reshape(level_windows, WPL, rows)
    labels = jnp.broadcast_to(labels[..., None], labels.shape + (WLON,)).reshape(positions, WIN)
    label_q = labels.reshape(positions, owners, WIN // owners).transpose(0, 2, 1).reshape(positions, WIN, 1)
    spare = WIN - LANES
    ends = jnp.tile(labels[:, LANES:], (1, head_count))
    ends = jnp.pad(ends, ((0, 0), (0, LANES - head_count * spare)), constant_values=-1)
    label_k = jnp.stack([labels[:, :LANES], ends], axis=1)
    dma = pltpu.SemaphoreType.DMA
    vmem, hbm = pl.BlockSpec(memory_space=pltpu.VMEM), pl.BlockSpec(memory_space=pl.ANY)
    smem = pl.BlockSpec(memory_space=pltpu.SMEM)
    cell = (rows, cols, levels, features)
    blk = (WIN, LANES)
    wide = (head_count + 1) * LANES
    down, dw = d_part.shape[1:]
    a_shape, d_shape = (height, features), (down, dw)
    sizes = [(owners * n, features) for n in (n_qkv, n_proj, n_up)] + [(features, 2 * dw)]
    v = pltpu.VMEM
    scratch = [v((2,) + cell, BF16), v((owners, 2) + a_shape, BF16), v((owners, 2) + d_shape, BF16),
               v((positions, owners) + blk, BF16)]
    lane_tiles = -(-features // LANES)
    scratch += [v((lane_tiles, rows * cols * levels, LANES), F32)] + [v((positions, WIN, features), F32)] * 3
    scratch += [v((lane_tiles, WIN, LANES), F32), v((owners * WIN, LANES), F32), v((head_count + 1,) + blk, F32)]
    scratch += [v((WIN, wide), BF16)] * 2 + [v((wide, features), BF16)] * 2
    scratch += [v((WIN // owners * SUB, LANES), F32)] * 2 + [v((positions, WIN // owners * SUB, LANES), F32)]
    scratch += [v(size, BF16) for size in sizes] + [v((2, features), F32)]
    scratch += [v(size, F32) for size in sizes] + [v((2, features), F32)]
    scratch += [v((2, owners) + a_shape, BF16), v((2, owners) + d_shape, BF16), v(cell, BF16)]
    scratch += [v((owners,) + s, BF16) for s in (a_shape, d_shape)] * 2
    scratch += [v((reach,) + s, BF16) for s in (a_shape, d_shape)] * 3
    scratch += [v((rows_n,) + s, BF16) for s in (a_shape, d_shape)] + [v((2,) + s, F32) for s in (a_shape, d_shape)]
    scratch += [v((positions, owners) + blk, BF16)] + [v((positions, reach) + blk, BF16)] * 3
    scratch += [v((nlat, positions) + blk, BF16), v((nlat * positions * WIN, LANES), F32)]
    scratch += [dma((2,))] + [dma((2, 3))] * 2 + [dma((2, reach))] * 4 + [dma((2, nlon))] * 2
    scratch += [dma((positions, reach))] * 8 + [dma((positions, rows_n))] * 4
    scratch += [dma((2,))] * 2 + [dma((2, reach))] * 4 + [dma((2, rows_n))] * 2 + [dma((2,))] * 2 + [dma((3,))] * 2
    outs = [(cell, BF16), ((n_qkv, features), F32), ((n_proj, features), F32), ((features, n_up), F32),
            ((down, 2 * dw), F32), ((2, gain_cols), F32), ((head_count, type_count, part), F32)]
    token_count = levels * rows * cols * nlat * nlon
    grad, qkv, proj, up, down_g, gain, table = pl.pallas_call(
        functools.partial(fused_kernel, nlat, nlon, (n_up, n_qkv, n_proj), 1.0 / math.sqrt(token_count)),
        out_shape=[jax.ShapeDtypeStruct(*o) for o in outs],
        in_specs=[hbm, hbm, vmem, vmem, vmem, smem, vmem, vmem],
        out_specs=[vmem] * len(outs),
        scratch_shapes=scratch,
        compiler_params=pltpu.CompilerParams(
            collective_id=0, has_side_effects=True, vmem_limit_bytes=56 * 2**20
        ),
    )(
        inputs.transpose(1, 2, 0, 3), cotangent.transpose(1, 2, 0, 3), a_part, d_part,
        bias_table.transpose(1, 0, 2), type_of, label_q, label_k,
    )
    return grad.transpose(2, 0, 1, 3), qkv.T, proj.T, up, down_g.T, gain, table.transpose(1, 0, 2)


def shards(*args):
    inputs, bias_table = args[0], args[7]
    nlat, nlon = lax.axis_size("lat"), lax.axis_size("lon")
    levels, rows, cols, _ = inputs.shape
    heads = bias_table.shape[1]
    whole_rows = bias_table.shape[2] * nlon == WIN * WIN and nlon == SUB and WIN % nlon == 0
    one_window = rows == WLAT and cols == WLON and levels == SUB and nlat % 2 == 0
    ends_fit = WIN > LANES and (WIN - LANES) * heads <= LANES and heads < SUB
    tiled = all(args[i].shape[1] % SUB == 0 for i in (2, 3, 4, 5))
    if whole_rows and one_window and ends_fit and tiled:
        return shards_fused(*args)
    return shards_plain(*args)


def solution(mesh):
    return jax.shard_map(
        shards,
        mesh=mesh,
        in_specs=(
            P(None, "lat", "lon", None),
            P(None, "lat", "lon", None),
            P(None, "lon"),
            P(None, "lon"),
            P(None, "lon"),
            P(None, "lon"),
            P(None, "lon"),
            P(None, None, "lon"),
            P(),
            P(None, "lat"),
        ),
        out_specs=(
            P(None, "lat", "lon", None),
            P(None, "lon"),
            P(None, "lon"),
            P(None, "lon"),
            P(None, "lon"),
            P(None, "lon"),
            P(None, None, "lon"),
        ),
        check_vma=False,
    )
```

```python
import functools
import math

import jax
import jax.numpy as jnp
from jax import lax
from jax.experimental import pallas as pl
from jax.experimental.pallas import tpu as pltpu
from jax.sharding import PartitionSpec as P

WPL = 2
WLAT = 6
WLON = 12
WIN = 144
MESH = pl.DeviceIdType.MESH
F32 = jnp.float32
BF16 = jnp.bfloat16


def layer_norm(values):
    row_mean = jnp.mean(values, axis=-1, keepdims=True)
    centred = values - row_mean
    variance = jnp.mean(centred * centred, axis=-1, keepdims=True)
    inv_std = lax.rsqrt(variance + 1e-05)
    return (centred * inv_std, inv_std)


def norm_back(d_normed, normed, inv_std):
    return inv_std * (
        d_normed
        - jnp.mean(d_normed, axis=-1, keepdims=True)
        - normed * jnp.mean(d_normed * normed, axis=-1, keepdims=True)
    )


def gelu_pair(pre_act):
    cumul = 0.5 * (1.0 + lax.erf(pre_act * 0.7071067811865476))
    density = jnp.exp(-0.5 * pre_act * pre_act) * 0.3989422804014327
    return (pre_act * cumul, cumul + pre_act * density)


def position(nlat, nlon):
    lat, lon = lax.axis_index("lat"), lax.axis_index("lon")

    def at(dlat, dlon):
        return (lax.rem(lat + dlat + nlat, nlat), lax.rem(lon + dlon + nlon, nlon))

    core, side = lax.rem(lat, 2), lax.rem(lon, 2)
    twin = (lat + 1 - 2 * core, lon)
    across = (lat, lon + 1 - 2 * side)
    return lat, lon, at, core, twin, across


def greet(devices):
    barrier = pltpu.get_barrier_semaphore()
    for device in devices:
        pl.semaphore_signal(barrier, inc=1, device_id=device, device_id_type=MESH)
    pl.semaphore_wait(barrier, len(devices))


def peers(nlat, nlon, at, twin, across):
    steps = [(0, d) for d in range(2, nlon, 2)] + [(d, 0) for d in range(2, nlat, 2)]
    steps += [(1, 0), (-1, 0), (0, 1), (0, -1), (1, 1), (-1, -1)]
    return [twin, across] + [at(*step) for step in steps]


def send(src, dst, send_sem, recv_sem, device):
    copy = pltpu.make_async_remote_copy(
        src_ref=src, dst_ref=dst, send_sem=send_sem, recv_sem=recv_sem, device_id=device, device_id_type=MESH
    )
    copy.start()
    return copy


def gather_kernel(nlat, nlon, a, d, b, h_lat, h_lon, h_diag, a_all, d_all, b_all, r_lat, r_lon, r_diag,
                  zs, zr, xs, xr, ts, tr, hs, hr):
    lat, lon, at, core, twin, across = position(nlat, nlon)
    greet(peers(nlat, nlon, at, twin, across))
    reach = nlon // 2
    srcs = (a.at[core], d.at[core], b)

    def slots(owner):
        return (a_all.at[owner, core], d_all.at[owner, core], b_all.at[owner])

    far, near, shared, halo = {}, {}, [], []
    for k in range(1, reach):
        for i in range(3):
            far[i, k] = send(srcs[i], slots(lon)[i], zs.at[i, k], zr.at[i, k], at(0, 2 * k))
    for i in range(3):
        near[i, 0] = send(srcs[i], slots(lon)[i], xs.at[i, 0], xr.at[i, 0], across)
    for i, (src, dst, step) in enumerate(
        ((h_lat, r_lat, (-1, 0)), (h_lon, r_lon, (0, -1)), (h_diag, r_diag, (-1, -1)))
    ):
        halo.append(send(src, dst, hs.at[i], hr.at[i], at(*step)))
    a_all[lon] = a[...]
    d_all[lon] = d[...]
    b_all[lon] = b[...]
    for k in range(1, reach):
        owner = lax.rem(lon - 2 * k + nlon, nlon)
        for i in range(3):
            slot = slots(owner)[i]
            far[i, k].wait_recv()
            near[i, k] = send(slot, slot, xs.at[i, k], xr.at[i, k], across)
            if i < 2:
                shared.append(send(slot, slot, ts.at[i, k], tr.at[i, k], twin))
    for k in range(reach):
        owner = lax.rem(across[1] - 2 * k + nlon, nlon)
        for i in range(3):
            slot = slots(owner)[i]
            near[i, k].wait_recv()
            if i < 2:
                shared.append(send(slot, slot, ts.at[i, reach + k], tr.at[i, reach + k], twin))
    for copy in list(far.values()) + list(near.values()):
        copy.wait_send()
    for copy in halo + shared:
        copy.wait()


def reduce_kernel(nlat, nlon, scale, a, d, t, kron, h_lat, h_lon, h_diag, a_out, d_out, t_out, r_lat, r_lon, r_diag,
                  a_twin, d_twin, a_half, d_half, a_x, d_x, t_x, a_mid, d_mid, t_mid, a_z, d_z, t_z,
                  a_row, d_row, t_row, cs, cr, xs, xr, zs, zr, ls, lr, fs, fr, hs, hr):
    lat, lon, at, core, twin, across = position(nlat, nlon)
    greet(peers(nlat, nlon, at, twin, across))
    reach = nlon // 2
    near, far, rest = {}, {}, []
    order = list(range(1, reach)) + [0]
    pairs = [
        send(src.at[1 - core], dst, cs.at[i], cr.at[i], twin)
        for i, (src, dst) in enumerate(((a, a_twin), (d, d_twin)))
    ]

    def cross(i, src, dst):
        for k in order:
            owner = lax.rem(across[1] + 2 * k, nlon)
            near[i, k] = send(src.at[owner], dst.at[k], xs.at[i, k], xr.at[i, k], across)

    cross(2, t, t_x)
    for i, (src, dst, step) in enumerate(
        ((h_lat, r_lat, (1, 0)), (h_lon, r_lon, (0, 1)), (h_diag, r_diag, (1, 1)))
    ):
        rest.append(send(src, dst, hs.at[i], hr.at[i], at(*step)))
    for i, (own, got, half, dst) in enumerate(((a, a_twin, a_half, a_x), (d, d_twin, d_half, d_x))):
        pairs[i].wait()
        half[...] = (own[core].astype(F32) + got[...].astype(F32)).astype(BF16)
        cross(i, half, dst)
    streams = ((2, t, t_x, t_mid, t_z), (0, a_half, a_x, a_mid, a_z), (1, d_half, d_x, d_mid, d_z))
    for i, own, got, mid, dst in streams:
        for k in range(1, reach):
            owner = lax.rem(lon + 2 * k, nlon)
            near[i, k].wait_recv()
            mid[k] = (own[owner].astype(F32) + got[k].astype(F32)).astype(BF16)
            far[i, k] = send(mid.at[k], dst.at[k], zs.at[i, k], zr.at[i, k], at(0, 2 * k))
    rows = nlat // 2
    row = lax.div(lat, 2)

    def total_of(i, own, got, dst):
        near[i, 0].wait_recv()
        total = own[lon].astype(F32) + got[0].astype(F32)
        for k in range(1, reach):
            far[i, k].wait_recv()
            total = total + dst[k].astype(F32)
        return total.astype(BF16)

    t_row[lat] = total_of(2, t, t_x, t_z)
    rest.append(send(t_row.at[lat], t_row.at[lat], ls.at[2, 0], lr.at[2, 0], twin))
    t_far = [send(t_row.at[lat], t_row.at[lat], ls.at[2, j], lr.at[2, j], at(2 * j, 0)) for j in range(1, rows)]
    halves = []
    for i, own, got, dst, line in ((0, a_half, a_x, a_z, a_row), (1, d_half, d_x, d_z, d_row)):
        line[row] = total_of(i, own, got, dst)
        halves.append(
            [send(line.at[row], line.at[row], ls.at[i, j], lr.at[i, j], at(2 * j, 0)) for j in range(1, rows)]
        )
    for j in range(1, rows):
        slot = t_row.at[lax.rem(lat - 2 * j + nlat, nlat)]
        t_far[j - 1].wait_recv()
        rest.append(send(slot, slot, fs.at[2, j], fr.at[2, j], twin))
    for i, (line, out) in enumerate(((a_row, a_out), (d_row, d_out))):
        for copy in halves[i]:
            copy.wait_recv()
        total = line[0].astype(F32)
        for j in range(1, rows):
            total = total + line[j].astype(F32)
        out[core] = total * scale
        rest.append(send(out.at[core], out.at[core], fs.at[i, 0], fr.at[i, 0], twin))
    for copy in list(near.values()) + list(far.values()) + t_far + halves[0] + halves[1]:
        copy.wait_send()
    for copy in rest:
        copy.wait()
    total = jnp.zeros(t_out.shape, F32)
    for i in range(nlat):
        total = total + jnp.dot(kron[i], t_row[i], preferred_element_type=F32)
    t_out[...] = total


def comm_call(kernel, collective_id, outs, scratch, operands):
    vmem = pl.BlockSpec(memory_space=pltpu.VMEM)
    return pl.pallas_call(
        kernel,
        out_shape=[jax.ShapeDtypeStruct(*o) for o in outs],
        in_specs=[vmem] * len(operands),
        out_specs=[vmem] * len(outs),
        scratch_shapes=scratch,
        compiler_params=pltpu.CompilerParams(
            collective_id=collective_id, has_side_effects=True, vmem_limit_bytes=48 * 2**20
        ),
    )(*operands)


def to_windows(grid):
    p, l, c = grid.shape[:3]
    shaped = grid.reshape(p // WPL, WPL, l // WLAT, WLAT, c // WLON, WLON, grid.shape[-1])
    return shaped.transpose(4, 0, 2, 1, 3, 5, 6).reshape(-1, grid.shape[-1])


def from_windows(flat, p, l, c):
    shaped = flat.reshape(c // WLON, p // WPL, l // WLAT, WPL, WLAT, WLON, flat.shape[-1])
    return shaped.transpose(1, 3, 2, 4, 0, 5, 6).reshape(p, l, c, flat.shape[-1])


def by_t(x, w_t):
    return lax.dot_general(x, w_t, (((1,), (1,)), ((), ())), preferred_element_type=F32)


def outer(x, y):
    return lax.dot_general(x, y, (((0,), (0,)), ((), ())), preferred_element_type=F32)


def plain(x, y):
    return jnp.dot(x, y, preferred_element_type=F32)


def pick_kernel(types, table, out):
    positions = types.shape[0]
    rows = [table[types[i]].astype(F32) for i in range(positions)]
    out[...] = jnp.concatenate(rows, axis=0).astype(BF16)


def pick_rows(types, table):
    _, head_count, part = table.shape
    return pl.pallas_call(
        pick_kernel,
        out_shape=jax.ShapeDtypeStruct((types.shape[0] * head_count, part), BF16),
        in_specs=[pl.BlockSpec(memory_space=pltpu.SMEM), pl.BlockSpec(memory_space=pltpu.VMEM)],
        out_specs=pl.BlockSpec(memory_space=pltpu.VMEM),
    )(types, table)


def window_kernel(n_up, n_qkv, n_proj, cells, cots, a_all, d_all, bias, label_col, label_row,
                  d_cells, ga, gd, table,
                  probs_s, qkv_t, proj_t, up_t, down_t, gains, g_qkv, g_proj, g_up, g_down, g_gain):
    owners, height = a_all.shape[0], a_all.shape[2]

    def joined(half, start, count):
        rows = [a_all[j, half].astype(F32)[start : start + count] for j in range(owners)]
        return jnp.concatenate(rows, axis=0).astype(BF16)

    up_t[...] = joined(0, 0, n_up)
    qkv_t[...] = joined(1, 0, n_qkv)
    proj_t[...] = joined(1, n_qkv, n_proj)
    wide = d_all.shape[3]
    for i in range(2):
        rows = [d_all[j, i].astype(F32) for j in range(owners)]
        down_t[:, i * wide : (i + 1) * wide] = jnp.concatenate(rows, axis=0).astype(BF16)
    gain_sum = a_all[0, 0].astype(F32)[n_up : n_up + 2]
    for j in range(1, owners):
        gain_sum = gain_sum + a_all[j, 0].astype(F32)[n_up : n_up + 2]
    gains[...] = gain_sum
    positions, head_count = bias.shape[:2]
    windows, _, features = cells.shape
    head_size = features // head_count
    factor = 1.0 / math.sqrt(head_size)
    for total in (g_qkv, g_proj, g_up, g_down, g_gain):
        total[...] = jnp.zeros(total.shape, F32)
    if windows > positions:
        table[...] = jnp.zeros(table.shape, F32)

    def body(w, carry):
        p = lax.rem(w, positions)
        gain_one, gain_two = gains[0:1], gains[1:2]
        lane_head = lax.broadcasted_iota(jnp.int32, (1, features), 1) // head_size
        heads = [(lane_head == h).astype(BF16) for h in range(head_count)]
        normed_one, inv_one = layer_norm(cells[w].astype(F32))
        scaled_one = (normed_one * gain_one).astype(BF16)
        q, k, v = (
            by_t(scaled_one, qkv_t[i * features : (i + 1) * features]).astype(BF16) for i in range(3)
        )
        same = label_col[p] == label_row[p]
        attended = jnp.zeros((WIN, features), F32)
        for h, head in enumerate(heads):
            scores = by_t(q * head, k) * factor + bias[p, h].astype(F32)
            scores = jnp.where(same, scores, -jnp.inf)
            raised = jnp.exp(scores - jnp.max(scores, axis=-1, keepdims=True))
            probs = raised * (1.0 / jnp.sum(raised, axis=-1, keepdims=True))
            probs_s[h] = probs
            attended = attended + plain(probs.astype(BF16), v * head)
        attended = attended.astype(BF16)
        middle = cells[w].astype(F32) + by_t(attended, proj_t[...])
        normed_two, inv_two = layer_norm(middle)
        scaled_two = (normed_two * gain_two).astype(BF16)
        cot = cots[w]
        activated, slope = gelu_pair(by_t(scaled_two, up_t[...]))
        g_down[...] += outer(cot, activated.astype(BF16))
        d_hidden = (plain(cot, down_t[...]) * slope).astype(BF16)
        g_up[...] += outer(d_hidden, scaled_two)
        d_htwo = plain(d_hidden, up_t[...])
        g_gain[1:2] += jnp.sum(d_htwo * normed_two, axis=0, keepdims=True)
        d_middle = cot.astype(F32) + norm_back(d_htwo * gain_two, normed_two, inv_two)
        d_middle_b = d_middle.astype(BF16)
        g_proj[...] += outer(d_middle_b, attended)
        d_att = plain(d_middle_b, proj_t[...]).astype(BF16)
        d_q, d_k, d_v = (jnp.zeros((WIN, features), F32) for _ in range(3))
        for h, head in enumerate(heads):
            probs, d_att_h = probs_s[h], d_att * head
            d_prob = by_t(d_att_h, v)
            d_v = d_v + outer(probs.astype(BF16), d_att_h)
            d_score = probs * (d_prob - jnp.sum(probs * d_prob, axis=-1, keepdims=True))
            if windows > positions:
                table[p, h] += d_score
            else:
                table[p, h] = d_score.astype(table.dtype)
            d_score_b = d_score.astype(BF16)
            d_q = d_q + plain(d_score_b, k * head)
            d_k = d_k + outer(d_score_b, q * head)
        d_hone = jnp.zeros((WIN, features), F32)
        for i, part in enumerate((d_q * factor, d_k * factor, d_v)):
            part = part.astype(BF16)
            span = slice(i * features, (i + 1) * features)
            g_qkv[span] += outer(part, scaled_one)
            d_hone = d_hone + plain(part, qkv_t[span])
        g_gain[0:1] += jnp.sum(d_hone * normed_one, axis=0, keepdims=True)
        d_cells[w] = (d_middle + norm_back(d_hone * gain_one, normed_one, inv_one)).astype(BF16)
        return carry

    lax.fori_loop(0, windows, body, 0)
    features = cells.shape[2]
    down = d_all.shape[2]
    gain_rows = jnp.concatenate([g_gain[...], jnp.zeros((height - n_up - 2, features), F32)], axis=0)
    spare = height - n_qkv - n_proj
    for j in range(owners):
        ga[0, j] = jnp.concatenate([g_up[j * n_up : (j + 1) * n_up], gain_rows], axis=0).astype(BF16)
        rows = [g_qkv[j * n_qkv : (j + 1) * n_qkv], g_proj[j * n_proj : (j + 1) * n_proj]]
        rows += [jnp.zeros((spare, features), F32)] if spare else []
        ga[1, j] = jnp.concatenate(rows, axis=0).astype(BF16)
        for i in range(2):
            gd[i, j] = g_down[j * down : (j + 1) * down, i * wide : (i + 1) * wide].astype(BF16)


def block_grads(cells, cots, a_all, d_all, cuts, bias, labels):
    features = cells.shape[1]
    positions, head_count = bias.shape[:2]
    windows, owners, wide = cells.shape[0] // WIN, a_all.shape[0], d_all.shape[3] * 2
    vmem = pl.BlockSpec(memory_space=pltpu.VMEM)
    outs = [((windows, WIN, features), BF16)]
    outs += [((2, owners) + x.shape[2:], BF16) for x in (a_all, d_all)]
    outs += [(bias.shape, F32 if windows > positions else BF16)]
    n_up, n_qkv, n_proj = cuts
    sizes = [(owners * n, features) for n in (n_qkv, n_proj, n_up)] + [(features, wide)]
    d_cells, *grads = pl.pallas_call(
        functools.partial(window_kernel, *cuts),
        out_shape=[jax.ShapeDtypeStruct(*o) for o in outs],
        in_specs=[vmem] * 7,
        out_specs=[vmem] * len(outs),
        scratch_shapes=[pltpu.VMEM((head_count, WIN, WIN), F32)]
        + [pltpu.VMEM(size, BF16) for size in sizes] + [pltpu.VMEM((2, features), F32)]
        + [pltpu.VMEM(size, F32) for size in sizes] + [pltpu.VMEM((2, features), F32)],
        compiler_params=pltpu.CompilerParams(vmem_limit_bytes=48 * 2**20),
    )(
        cells.reshape(windows, WIN, features), cots.reshape(windows, WIN, features),
        a_all, d_all, bias, labels[:, :, None], labels[:, None, :],
    )
    return (d_cells.reshape(cells.shape), *grads)


def shards_plain(inputs, cotangent, qkv_weight, proj_weight, up_weight, down_weight, norm_gains, bias_table, type_of, region):
    levels, rows, cols, features = inputs.shape
    nlat, nlon = lax.axis_size("lat"), lax.axis_size("lon")
    level_windows, row_windows = levels // WPL, rows // WLAT
    type_count, head_count, part = bias_table.shape
    positions = level_windows * row_windows
    lat_index = lax.axis_index("lat")
    row_half, col_half, level_shift = WLAT // 2, WLON // 2, WPL // 2
    all_types = type_of.reshape(level_windows, nlat, row_windows).transpose(1, 0, 2).reshape(nlat, positions)
    types = lax.dynamic_index_in_dim(all_types, lat_index, 0, keepdims=False)
    n_up, n_qkv, n_proj = up_weight.shape[1], qkv_weight.shape[1], proj_weight.shape[1]
    gain_cols, height = norm_gains.shape[1], -(-max(n_up + 2, n_qkv + n_proj) // 8) * 8
    gain_spot = lax.axis_index("lon") * gain_cols
    own_lane = jnp.arange(features, dtype=jnp.int32) // gain_cols == lax.axis_index("lon")
    gain_rows = jnp.where(own_lane, jnp.tile(norm_gains, (1, nlon)), jnp.zeros((), BF16))
    gain_rows = jnp.pad(gain_rows, ((0, height - n_up - 2), (0, 0)))
    a_part = jnp.stack(
        [
            jnp.concatenate([up_weight.T, gain_rows]),
            jnp.pad(
                jnp.concatenate([qkv_weight.T, proj_weight.T]), ((0, height - n_qkv - n_proj), (0, 0))
            ),
        ]
    )
    d_part = down_weight.reshape(2, -1, down_weight.shape[1]).transpose(0, 2, 1)
    b_part = pick_rows(types, bias_table)
    both = jnp.roll(jnp.stack([inputs, cotangent]), -level_shift, axis=1)
    rim_lat = both[:, :, :row_half, col_half:]
    rim_lon = both[:, :, row_half:, :col_half]
    rim_diag = both[:, :, :row_half, :col_half]
    flat = [r.reshape(-1, features) for r in (rim_lat, rim_lon, rim_diag)]
    dma = pltpu.SemaphoreType.DMA
    a_all, d_all, b_all, r_lat, r_lon, r_diag = comm_call(
        functools.partial(gather_kernel, nlat, nlon),
        0,
        [((nlon,) + x.shape, BF16) for x in (a_part, d_part, b_part)] + [(x.shape, BF16) for x in flat],
        [dma((3, nlon // 2))] * 4 + [dma((2, nlon))] * 2 + [dma((3,))] * 2,
        (a_part, d_part, b_part, *flat),
    )
    bias = b_all.transpose(1, 0, 2).reshape(positions, head_count, WIN, WIN)
    top = jnp.concatenate([both[:, :, row_half:, col_half:], r_lon.reshape(rim_lon.shape)], axis=3)
    bottom = jnp.concatenate([r_lat.reshape(rim_lat.shape), r_diag.reshape(rim_diag.shape)], axis=3)
    shifted = jnp.concatenate([top, bottom], axis=2)
    labels = region.reshape(level_windows, WPL, row_windows, WLAT).transpose(0, 2, 1, 3)
    labels = jnp.broadcast_to(labels[..., None], labels.shape + (WLON,)).reshape(positions, WIN)
    d_cells, ga, gd, table = block_grads(
        to_windows(shifted[0]), to_windows(shifted[1]), a_all, d_all, (n_up, n_qkv, n_proj), bias, labels
    )
    gt = table.astype(BF16).reshape(positions * head_count, nlon, part).transpose(1, 0, 2)
    onehot = (all_types[:, None, :] == jnp.arange(type_count, dtype=jnp.int32)[None, :, None]).astype(BF16)
    kron = jnp.einsum("lyp,gh->lygph", onehot, jnp.eye(head_count, dtype=BF16)).reshape(
        nlat, type_count * head_count, positions * head_count
    )
    back = from_windows(d_cells, levels, rows, cols)
    out_lat = back[:, rows - row_half :, : cols - col_half]
    out_lon = back[:, : rows - row_half, cols - col_half :]
    out_diag = back[:, rows - row_half :, cols - col_half :]
    flat = [r.reshape(-1, features) for r in (out_lat, out_lon, out_diag)]
    shard_shapes = (ga.shape[2:], gd.shape[2:], gt.shape[1:])
    token_count = levels * rows * cols * nlat * nlon
    a_sum, d_sum, t_sum, r_lat, r_lon, r_diag = comm_call(
        functools.partial(reduce_kernel, nlat, nlon, 1.0 / math.sqrt(token_count)),
        1,
        [((2,) + ga.shape[2:], F32), ((2,) + gd.shape[2:], F32), ((type_count * head_count, part), F32)]
        + [(x.shape, BF16) for x in flat],
        [pltpu.VMEM(x.shape[1:], BF16) for x in (ga, gd)] * 2
        + [pltpu.VMEM((nlon // 2,) + shape, BF16) for shape in shard_shapes] * 3
        + [pltpu.VMEM((nlat // 2,) + shape, BF16) for shape in shard_shapes[:2]]
        + [pltpu.VMEM((nlat,) + shard_shapes[2], BF16)]
        + [dma((2,))] * 2 + [dma((3, nlon // 2))] * 4 + [dma((3, nlat // 2))] * 4 + [dma((3,))] * 2,
        (ga, gd, gt, kron, *flat),
    )
    own = back[:, : rows - row_half, : cols - col_half]
    top = jnp.concatenate([r_diag.reshape(out_diag.shape), r_lat.reshape(out_lat.shape)], axis=2)
    bottom = jnp.concatenate([r_lon.reshape(out_lon.shape), own], axis=2)
    grad_input = jnp.roll(jnp.concatenate([top, bottom], axis=1), level_shift, axis=0)
    return (
        grad_input,
        a_sum[1, :n_qkv].T,
        a_sum[1, n_qkv : n_qkv + n_proj].T,
        a_sum[0, :n_up].T,
        d_sum.transpose(0, 2, 1).reshape(down_weight.shape),
        lax.dynamic_slice(a_sum[0, n_up : n_up + 2], (jnp.int32(0), gain_spot), (2, gain_cols)),
        t_sum.reshape(type_count, head_count, part),
    )


LANES = 128
SUB = 8


def rc(src, dst, send_sem, recv_sem, device):
    return pltpu.make_async_remote_copy(
        src_ref=src, dst_ref=dst, send_sem=send_sem, recv_sem=recv_sem, device_id=device, device_id_type=MESH
    )


def all_peers(nlat, nlon, at, across):
    steps = [(0, d) for d in range(2, nlon, 2)] + [(d, 0) for d in range(1, nlat)]
    steps += [(0, 1), (0, -1), (1, 1), (-1, -1)]
    return [across] + [at(*step) for step in steps]


def finish_kernel(*refs):
    count = (len(refs) - 1) // 3
    srcs, dsts, held, sems = refs[:count], refs[count : 2 * count], refs[2 * count : -1], refs[-1]
    loads = [pltpu.make_async_copy(srcs[i], held[i], sems.at[0, i]) for i in range(count)]
    stores = [pltpu.make_async_copy(held[i], dsts[i], sems.at[1, i]) for i in range(count)]
    for copy in loads:
        copy.start()
    for load, copy in zip(loads, stores):
        load.wait()
        copy.start()
    for copy in stores:
        copy.wait()


def fused_kernel(nlat, nlon, cuts, scale, x_in, c_in, qkv_in, proj_in, up_in, down_in, gain_in, tab_in, types, region,
                 out, qkv_o, proj_o, up_o, down_o, gain_o, t_out,
                 qkv_v, proj_v, up_v, down_v, gain_v, tab,
                 grid, a_all, d_all, b_all,
                 wide_s, cells_s, cots_s, dcell_s, perm_s, asm_s, score_s, prob_b, ds_b, kexp_s, vexp_s,
                 pick_m, pick_t, pick_u,
                 qkv_t, proj_t, up_t, down_t, gains, g_qkv, g_proj, g_up, g_down, g_gain,
                 ga, gd, obuf, a_twin, d_twin, a_half, d_half, a_x, d_x, a_mid, d_mid, a_z, d_z, a_row, d_row,
                 t_w, t_x, t_mid, t_z, t_row, t_val,
                 in_s, own_s, hs, hr, wzs, wzr, wxs, wxr, wts, wtr, bzs, bzr, bxs, bxr,
                 txs, txr, tzs, tzr, tls, tlr,
                 pcs, pcr, pxs, pxr, pzs, pzr, pls, plr, ohs, ohr):
    n_up, n_qkv, n_proj = cuts
    lat, lon, at, core, twin, across = position(nlat, nlon)
    rows_c, cols_c, levels, features = x_in.shape
    half_r, half_c = rows_c // 2, cols_c // 2
    head_count = tab.shape[0]
    type_count = tab.shape[1]
    positions = types.shape[0]
    owners, height, wide = nlon, a_all.shape[2], d_all.shape[3]
    lines_qp, lines_up = (n_qkv + n_proj) // 2, n_up // 2
    packed_qp, packed_up = lines_qp * 3 // 2, lines_up * 3 // 2
    side = features - LANES
    beats = head_count + 1
    span_b = b_all.shape[2]
    reach, rows_n = nlon // 2, nlat // 2
    head_size = features // head_count
    per = WIN // owners
    spare = WIN - LANES
    factor = 1.0 / math.sqrt(head_size)
    slab = WIN // WPL

    loads = [
        pltpu.make_async_copy(src, dst, in_s.at[i])
        for i, (src, dst) in enumerate(
            ((qkv_in, qkv_v), (proj_in, proj_v), (up_in, up_v), (gain_in, gain_v), (tab_in, tab), (down_in, down_v))
        )
    ]
    for copy in loads:
        copy.start()

    tiles = [(t, t * LANES, min(LANES, features - t * LANES)) for t in range(-(-features // LANES))]

    def fill(ref, value):
        for t, start, count in tiles:
            ref[t, :, :count] = value[:, start : start + count]

    def whole(ref):
        return jnp.concatenate([ref[t][:, :count] for t, _, count in tiles], axis=1)

    def strided(ref, start, size, stride):
        return jnp.concatenate(
            [ref.at[t][pl.ds(start, size, stride=stride), :][:, :count] for t, _, count in tiles], axis=1
        )

    def store_strided(ref, start, size, stride, value):
        for t, first, count in tiles:
            piece = value[:, first : first + count]
            if count < LANES:
                piece = jnp.concatenate([piece, jnp.zeros((size, LANES - count), F32)], axis=1)
            ref.at[t][pl.ds(start, size, stride=stride), :] = piece

    def pack(block):
        half = block.shape[0] // 2
        return jnp.concatenate(
            [block[:, :LANES], jnp.concatenate([block[:half, LANES:], block[half:, LANES:]], axis=1)], axis=0
        )

    def unpack(block):
        count = block.shape[0] * 2 // 3
        tail = jnp.concatenate([block[count:, :side], block[count:, side:]], axis=0)
        return jnp.concatenate([block[:count], tail], axis=1)

    lo_r, hi_r = pl.ds(0, half_r), pl.ds(half_r, rows_c - half_r)
    lo_c, hi_c = pl.ds(0, half_c), pl.ds(half_c, cols_c - half_c)
    end_r, end_c = pl.ds(rows_c - half_r, half_r), pl.ds(cols_c - half_c, half_c)
    first_r, first_c = pl.ds(0, rows_c - half_r), pl.ds(0, cols_c - half_c)

    def halo(g, i):
        src = (x_in, c_in)[g]
        dst = grid.at[g]
        if i == 0:
            return rc(src.at[lo_r, hi_c], dst.at[end_r, first_c], hs.at[g, i], hr.at[g, i], at(-1, 0))
        if i == 1:
            return rc(src.at[hi_r, lo_c], dst.at[first_r, end_c], hs.at[g, i], hr.at[g, i], at(0, -1))
        return rc(src.at[lo_r, lo_c], dst.at[end_r, end_c], hs.at[g, i], hr.at[g, i], at(-1, -1))

    def own(g):
        return pltpu.make_async_copy((x_in, c_in)[g].at[hi_r, hi_c], grid.at[g].at[first_r, first_c], own_s.at[g])

    for g in (0, 1):
        own(g).start()

    top = packed_qp + SUB

    def w_slot(i, owner):
        if i == 2:
            return d_all.at[owner, core]
        return a_all.at[owner, core].at[pl.ds(0, top) if i == 0 else pl.ds(top, packed_up)]

    def far_w(i, k):
        return rc(w_slot(i, lon), w_slot(i, lon), wzs.at[i, k], wzr.at[i, k], at(0, 2 * k))

    def near_w(i, k, owner):
        return rc(w_slot(i, owner), w_slot(i, owner), wxs.at[i, k], wxr.at[i, k], across)

    def pair_w(i, k, owner):
        return rc(w_slot(i, owner), w_slot(i, owner), wts.at[i, k], wtr.at[i, k], twin)

    def send_w(i):
        for k in range(1, reach):
            far_w(i, k).start()
        near_w(i, 0, lon).start()

    def pass_far(i):
        for k in range(1, reach):
            owner = lax.rem(lon - 2 * k + nlon, nlon)
            far_w(i, k).wait_recv()
            near_w(i, k, owner).start()
            pair_w(i, k, owner).start()

    def pass_near(i):
        for k in range(reach):
            owner = lax.rem(across[1] - 2 * k + nlon, nlon)
            near_w(i, k, owner).wait_recv()
            pair_w(i, reach + k, owner).start()

    def end_pair(i):
        for k in range(1, 2 * reach):
            pair_w(i, k, lon).wait_recv()

    greet(all_peers(nlat, nlon, at, across))
    for i in range(3):
        halo(0, i).start()
    for copy in loads[:4]:
        copy.wait()
    both = jnp.concatenate([qkv_v[...].astype(F32), proj_v[...].astype(F32)], axis=0)
    first = up_v[...].astype(F32).T
    gain_v32 = gain_v[...].astype(F32)
    gain_rows = jnp.concatenate([gain_v32, jnp.zeros((2, LANES - gain_v32.shape[1]), F32)], axis=1)
    gain_rows = jnp.concatenate([gain_rows, jnp.zeros((SUB - 2, LANES), F32)], axis=0)
    for i in range(2):
        a_all[lon, i] = jnp.concatenate(
            [
                pack(both[i * lines_qp : (i + 1) * lines_qp]),
                gain_rows,
                pack(first[i * lines_up : (i + 1) * lines_up]),
            ],
            axis=0,
        ).astype(BF16)
    send_w(0)
    loads[4].wait()

    rows_i = lax.broadcasted_iota(jnp.int32, (SUB, type_count), 0)
    want = jnp.full((SUB, type_count), -1, jnp.int32)
    for i in range(positions):
        want = jnp.where(rows_i == i, types[i, lat], want)
    onehot = (lax.broadcasted_iota(jnp.int32, (SUB, type_count), 1) == want).astype(F32).astype(BF16)
    tails = [jnp.zeros((per, LANES), F32) for _ in range(positions)]
    for h in range(head_count):
        val = jnp.dot(onehot, tab[h], preferred_element_type=F32)
        for r in range(per):
            pick_m[r * SUB : (r + 1) * SUB] = val[:, r * WIN : r * WIN + LANES]
            end = val[:, r * WIN + LANES : (r + 1) * WIN]
            pick_t[r * SUB : (r + 1) * SUB] = jnp.concatenate([end, jnp.zeros((SUB, LANES - spare), F32)], axis=1)
        for i in range(positions):
            pick_u[i, pl.ds(h, per, stride=beats), :] = pick_m[pl.ds(i, per, stride=SUB), :]
            piece = pick_t[pl.ds(i, per, stride=SUB), :]
            tails[i] = tails[i] + (pltpu.roll(piece, h * spare, 1) if h else piece)
    for i in range(positions):
        pick_u[i, pl.ds(head_count, per, stride=beats), :] = tails[i]
        pick_u[i, per * beats :, :] = jnp.zeros((span_b - per * beats, LANES), F32)

    def far_b(p, k):
        return rc(b_all.at[p, lon], b_all.at[p, lon], bzs.at[p, k], bzr.at[p, k], at(0, 2 * k))

    def relay_b(p):
        rc(b_all.at[p, lon], b_all.at[p, lon], bxs.at[p, 0], bxr.at[p, 0], across).start()
        for k in range(1, reach):
            far_b(p, k).wait_recv()
            slot = b_all.at[p, lax.rem(lon - 2 * k + nlon, nlon)]
            rc(slot, slot, bxs.at[p, k], bxr.at[p, k], across).start()

    def near_b(p, k):
        slot = b_all.at[p, lon]
        return rc(slot, slot, bxs.at[p, k], bxr.at[p, k], across)

    for i in range(positions):
        b_all[i, lon] = pick_u[i].astype(BF16)

    def send_b(p):
        for k in range(1, reach):
            far_b(p, k).start()

    send_b(0)
    loads[5].wait()
    for i in range(2):
        d_all[lon, i] = down_v[:, i * wide : (i + 1) * wide]
    send_w(1)
    send_w(2)
    for i in range(3):
        halo(1, i).start()
    for i in range(1, positions):
        send_b(i)

    def windows_of(g, store):
        own(g).wait()
        for i in range(3):
            halo(g, i).wait_recv()
        fill(wide_s, grid[g].astype(F32).reshape(rows_c * cols_c * levels, features))
        for i in range(positions):
            for j in range(WPL):
                level = (WPL * i + j + WPL // 2) % levels
                store[i, j * slab : (j + 1) * slab] = strided(wide_s, level, slab, levels)

    for total in (g_qkv, g_proj, g_up, g_down, g_gain):
        total[...] = jnp.zeros(total.shape, F32)
    asm_s[...] = jnp.zeros(asm_s.shape, F32)
    pass_far(0)
    relay_b(0)
    windows_of(0, cells_s)
    pass_near(0)
    pass_far(1)
    pass_far(2)
    end_pair(0)
    for j in range(owners):
        rows = [unpack(a_all[j, i, :packed_qp].astype(F32)) for i in range(2)]
        rows = jnp.concatenate(rows, axis=0).astype(BF16)
        qkv_t[j * n_qkv : (j + 1) * n_qkv] = rows[:n_qkv]
        proj_t[j * n_proj : (j + 1) * n_proj] = rows[n_qkv:]
    lanes = features // owners
    gains[...] = jnp.concatenate(
        [a_all[j, 0, packed_qp:top].astype(F32)[:2, :lanes] for j in range(owners)], axis=1
    )

    def late_weights():
        pass_near(1)
        pass_near(2)
        windows_of(1, cots_s)
        end_pair(1)
        end_pair(2)
        for j in range(owners):
            rows = [unpack(a_all[j, i, top:].astype(F32)) for i in range(2)]
            up_t[j * n_up : (j + 1) * n_up] = jnp.concatenate(rows, axis=0).astype(BF16)
        for i in range(2):
            rows = [d_all[j, i].astype(F32) for j in range(owners)]
            down_t[:, i * wide : (i + 1) * wide] = jnp.concatenate(rows, axis=0).astype(BF16)

    def near_t(p, k):
        owner = lax.rem(across[1] + 2 * k, nlon)
        return rc(t_w.at[p, owner], t_x.at[p, k], txs.at[p, k], txr.at[p, k], across)

    def far_t(p, k):
        return rc(t_mid.at[p, k], t_z.at[p, k], tzs.at[p, k], tzr.at[p, k], at(0, 2 * k))

    order = list(range(1, reach)) + [0]

    def stage_one(p):
        for k in order:
            near_t(p, k).start()

    def stage_two(p):
        for k in range(1, reach):
            owner = lax.rem(lon + 2 * k, nlon)
            near_t(p, k).wait_recv()
            t_mid[p, k] = (t_w[p, owner].astype(F32) + t_x[p, k].astype(F32)).astype(BF16)
            far_t(p, k).start()

    def row_t(p, j):
        slot = t_row.at[lat, p]
        return rc(slot, slot, tls.at[p, j], tlr.at[p, j], at(j, 0))

    def stage_three(p):
        near_t(p, 0).wait_recv()
        total = t_w[p, lon].astype(F32) + t_x[p, 0].astype(F32)
        for k in range(1, reach):
            far_t(p, k).wait_recv()
            total = total + t_z[p, k].astype(F32)
        t_row[lat, p] = total.astype(BF16)
        for j in range(1, nlat):
            row_t(p, j).start()

    lane_head = lax.broadcasted_iota(jnp.int32, (1, features), 1) // head_size
    seg = lax.broadcasted_iota(jnp.int32, (1, LANES), 1) // spare

    def to_perm(value):
        fill(perm_s, value)
        return jnp.concatenate([strided(perm_s, r, SUB, per) for r in range(per)], axis=0)

    def from_perm(value):
        for r in range(per):
            store_strided(perm_s, r, SUB, per, value[r * SUB : (r + 1) * SUB])
        return whole(perm_s)

    def expand(dst, rows):
        low = rows[:LANES]
        high = rows[LANES:]
        ends = []
        for h in range(head_count):
            mine = lane_head == h
            dst[h * LANES : (h + 1) * LANES] = jnp.where(mine, low, 0.0).astype(BF16)
            ends.append(jnp.where(mine, high, 0.0))
        ends.append(jnp.zeros((LANES - head_count * spare, features), F32))
        dst[head_count * LANES :] = jnp.concatenate(ends, axis=0).astype(BF16)

    def collapse(big):
        low = big[:LANES]
        start = head_count * LANES
        high = big[start : start + spare]
        for h in range(1, head_count):
            mine = lane_head == h
            low = jnp.where(mine, big[h * LANES : (h + 1) * LANES], low)
            high = jnp.where(mine, big[start + h * spare : start + (h + 1) * spare], high)
        return jnp.concatenate([low, high], axis=0)

    def block(h):
        return slice(h * LANES, (h + 1) * LANES)

    token_k = lax.broadcasted_iota(jnp.int32, (1, LANES), 1)
    token_end = LANES + token_k - spare * seg
    place_q = lax.broadcasted_iota(jnp.int32, (WIN, 1), 0)
    turn_q = place_q >> (SUB.bit_length() - 1)
    token_q = per * (place_q - SUB * turn_q) + turn_q
    cells_r = rows_c * WPL

    def label_of(p, token):
        label = jnp.full(token.shape, region[WPL * p, 0], jnp.int32)
        for g in range(1, cells_r):
            label = jnp.where(token >= cols_c * g, region[WPL * p + g // rows_c, g % rows_c], label)
        return label

    def body(p, carry):
        gain_one, gain_two = gains[0:1], gains[1:2]
        normed_one, inv_one = layer_norm(cells_s[p])
        scaled_one = (normed_one * gain_one).astype(BF16)
        q, k, v = (by_t(scaled_one, qkv_t[i * features : (i + 1) * features]) for i in range(3))
        qp = to_perm(q).astype(BF16)
        expand(kexp_s, k)
        expand(vexp_s, v)
        for j in range(reach):
            near_b(p, j).wait_recv()
        for j in range(owners):
            asm_s[j * span_b : (j + 1) * span_b] = b_all[p, j].astype(F32)
        mine_q = label_of(p, token_q)
        same = mine_q == label_of(p, token_k)
        same_end = mine_q == jnp.where(seg < head_count, label_of(p, token_end), -1)

        def bias_of(h):
            return jnp.concatenate([asm_s[pl.ds(r * beats + h, SUB, stride=span_b), :] for r in range(per)], axis=0)

        def raw(h, keep):
            scores = by_t(qp, kexp_s[block(h)]) * factor + bias_of(h)
            return jnp.where(keep, scores, -jnp.inf)

        last = head_count
        s_end = raw(last, same_end)
        peak_end = jnp.zeros((WIN, LANES), F32)
        for h in range(head_count):
            mine = seg == h
            s = raw(h, same)
            peak = jnp.max(jnp.maximum(s, jnp.where(mine, s_end, -jnp.inf)), axis=-1, keepdims=True)
            score_s[h] = jnp.exp(s - peak)
            peak_end = jnp.where(mine, peak, peak_end)
        e_end = jnp.exp(s_end - peak_end)
        inv_end = jnp.zeros((WIN, LANES), F32)
        for h in range(head_count):
            mine = seg == h
            e = score_s[h]
            inv = 1.0 / jnp.sum(e + jnp.where(mine, e_end, 0.0), axis=-1, keepdims=True)
            probs = e * inv
            score_s[h] = probs
            prob_b[:, block(h)] = probs.astype(BF16)
            inv_end = jnp.where(mine, inv, inv_end)
        p_end = e_end * inv_end
        score_s[last] = p_end
        prob_b[:, block(last)] = p_end.astype(BF16)
        attended = from_perm(plain(prob_b[...], vexp_s[...])).astype(BF16)

        @pl.when(p == 0)
        def _():
            late_weights()
            if positions > 1:
                relay_b(1)

        middle = cells_s[p] + by_t(attended, proj_t[...])
        normed_two, inv_two = layer_norm(middle)
        scaled_two = (normed_two * gain_two).astype(BF16)
        cot = cots_s[p].astype(BF16)
        activated, slope = gelu_pair(by_t(scaled_two, up_t[...]))
        g_down[...] += outer(cot, activated.astype(BF16))
        d_hidden = (plain(cot, down_t[...]) * slope).astype(BF16)
        g_up[...] += outer(d_hidden, scaled_two)
        d_htwo = plain(d_hidden, up_t[...])
        g_gain[1:2] += jnp.sum(d_htwo * normed_two, axis=0, keepdims=True)
        d_middle = cots_s[p] + norm_back(d_htwo * gain_two, normed_two, inv_two)
        d_middle_b = d_middle.astype(BF16)
        g_proj[...] += outer(d_middle_b, attended)
        dap = to_perm(plain(d_middle_b, proj_t[...])).astype(BF16)

        p_end = score_s[last]
        dp_end = by_t(dap, vexp_s[block(last)])
        mix_end = p_end * dp_end
        dot_end = jnp.zeros((WIN, LANES), F32)

        def put(h, ds):
            ds_b[:, block(h)] = ds.astype(BF16)
            for r in range(per):
                asm_s[pl.ds(r * beats + h, SUB, stride=span_b), :] = ds[r * SUB : (r + 1) * SUB]

        for h in range(head_count):
            mine = seg == h
            probs = score_s[h]
            dp = by_t(dap, vexp_s[block(h)])
            dot = jnp.sum(probs * dp + jnp.where(mine, mix_end, 0.0), axis=-1, keepdims=True)
            dot_end = jnp.where(mine, dot, dot_end)
            put(h, probs * (dp - dot))
        put(last, p_end * (dp_end - dot_end))
        for j in range(owners):
            t_w[p, j] = asm_s[j * span_b : (j + 1) * span_b].astype(BF16)
        stage_one(p)
        d_q = from_perm(plain(ds_b[...], kexp_s[...]))
        d_k = collapse(outer(ds_b[...], qp))
        d_v = collapse(outer(prob_b[...], dap))
        d_hone = jnp.zeros((WIN, features), F32)
        for i, part in enumerate((d_q * factor, d_k * factor, d_v)):
            part = part.astype(BF16)
            span = slice(i * features, (i + 1) * features)
            g_qkv[span] += outer(part, scaled_one)
            d_hone = d_hone + plain(part, qkv_t[span])
        g_gain[0:1] += jnp.sum(d_hone * normed_one, axis=0, keepdims=True)
        dcell_s[p] = d_middle + norm_back(d_hone * gain_one, normed_one, inv_one)

        @pl.when(p + 2 < positions)
        def _():
            relay_b(p + 2)

        @pl.when(p >= 1)
        def _():
            stage_two(p - 1)

        @pl.when(p >= 2)
        def _():
            stage_three(p - 2)

        return carry

    lax.fori_loop(0, positions, body, 0)

    down = d_all.shape[2]
    no_gain = jnp.zeros((SUB, LANES), F32)
    for j in range(owners):
        block_qp = jnp.concatenate(
            [g_qkv[j * n_qkv : (j + 1) * n_qkv], g_proj[j * n_proj : (j + 1) * n_proj]], axis=0
        )
        block_up = g_up[j * n_up : (j + 1) * n_up]
        own_gain = jnp.concatenate([g_gain[:, j * lanes : (j + 1) * lanes], jnp.zeros((2, LANES - lanes), F32)], axis=1)
        own_gain = jnp.concatenate([own_gain, jnp.zeros((SUB - 2, LANES), F32)], axis=0)
        for i in range(2):
            ga[i, j] = jnp.concatenate(
                [
                    pack(block_qp[i * lines_qp : (i + 1) * lines_qp]),
                    no_gain if i else own_gain,
                    pack(block_up[i * lines_up : (i + 1) * lines_up]),
                ],
                axis=0,
            ).astype(BF16)
            gd[i, j] = g_down[j * down : (j + 1) * down, i * wide : (i + 1) * wide].astype(BF16)
    pairs = [
        rc(src.at[1 - core], dst, pcs.at[i], pcr.at[i], twin)
        for i, (src, dst) in enumerate(((ga, a_twin), (gd, d_twin)))
    ]
    for copy in pairs:
        copy.start()
    for i in range(positions):
        for j in range(WPL):
            level = (WPL * i + j + WPL // 2) % levels
            store_strided(wide_s, level, slab, levels, dcell_s[i, j * slab : (j + 1) * slab])
    obuf[...] = whole(wide_s).reshape(obuf.shape).astype(BF16)
    outs = [
        rc(obuf.at[end_r, first_c], out.at[lo_r, hi_c], ohs.at[0], ohr.at[0], at(1, 0)),
        rc(obuf.at[first_r, end_c], out.at[hi_r, lo_c], ohs.at[1], ohr.at[1], at(0, 1)),
        rc(obuf.at[end_r, end_c], out.at[lo_r, lo_c], ohs.at[2], ohr.at[2], at(1, 1)),
    ]
    out[hi_r, hi_c] = obuf[first_r, first_c]
    halves = (a_half, d_half)
    p_x, p_mid, p_z = (a_x, d_x), (a_mid, d_mid), (a_z, d_z)

    def near_p(i, k):
        owner = lax.rem(across[1] + 2 * k, nlon)
        return rc(halves[i].at[owner], p_x[i].at[k], pxs.at[i, k], pxr.at[i, k], across)

    def far_p(i, k):
        return rc(p_mid[i].at[k], p_z[i].at[k], pzs.at[i, k], pzr.at[i, k], at(0, 2 * k))

    for i, (mine, got) in enumerate(((ga, a_twin), (gd, d_twin))):
        pairs[i].wait()
        halves[i][...] = (mine[core].astype(F32) + got[...].astype(F32)).astype(BF16)
        for k in order:
            near_p(i, k).start()
    for copy in outs:
        copy.start()
    for p in range(max(positions - 1, 0), positions):
        stage_two(p)
    for p in range(max(positions - 2, 0), positions - 1):
        stage_three(p)
    for i in (0, 1):
        for k in range(1, reach):
            owner = lax.rem(lon + 2 * k, nlon)
            near_p(i, k).wait_recv()
            p_mid[i][k] = (halves[i][owner].astype(F32) + p_x[i][k].astype(F32)).astype(BF16)
            far_p(i, k).start()
    stage_three(positions - 1)
    lines = (a_row, d_row)

    def line_p(i, j):
        slot = lines[i].at[lat]
        return rc(slot, slot, pls.at[i, j], plr.at[i, j], at(j, 0))

    for i in (0, 1):
        near_p(i, 0).wait_recv()
        total = halves[i][lon].astype(F32) + p_x[i][0].astype(F32)
        for k in range(1, reach):
            far_p(i, k).wait_recv()
            total = total + p_z[i][k].astype(F32)
        lines[i][lat] = total.astype(BF16)
        for j in range(1, nlat):
            line_p(i, j).start()
    for p in range(positions):
        for j in range(1, nlat):
            row_t(p, j).wait_recv()
    spots = nlat * positions
    for i in range(nlat):
        for p in range(positions):
            t_val[(i * positions + p) * span_b : (i * positions + p + 1) * span_b] = t_row[i, p].astype(F32)
    cols_i = lax.broadcasted_iota(jnp.int32, (type_count, spots), 1)
    want = jnp.full((type_count, spots), -1, jnp.int32)
    for i in range(nlat):
        for p in range(positions):
            want = jnp.where(cols_i == i * positions + p, types[p, i], want)
    by_type = (lax.broadcasted_iota(jnp.int32, (type_count, spots), 0) == want).astype(F32).astype(BF16)
    ends = [t_val[pl.ds(r * beats + head_count, spots, stride=span_b), :] for r in range(per)]
    for h in range(head_count):
        pieces = []
        for r in range(per):
            pieces.append(t_val[pl.ds(r * beats + h, spots, stride=span_b), :])
            pieces.append(ends[r][:, h * spare : (h + 1) * spare])
        flat = jnp.concatenate(pieces, axis=1).astype(BF16)
        t_out[h] = jnp.dot(by_type, flat, preferred_element_type=F32)
    def total_p(i, half):
        total = lines[i][half].astype(F32)
        for j in range(1, rows_n):
            total = total + lines[i][2 * j + half].astype(F32)
        return total * scale

    for i in (0, 1):
        for j in range(1, nlat):
            line_p(i, j).wait_recv()
    sums = [total_p(0, half) for half in range(2)]
    up_o[...] = jnp.concatenate([unpack(part[top:]) for part in sums], axis=0).T
    block_qp = jnp.concatenate([unpack(part[:packed_qp]) for part in sums], axis=0)
    qkv_o[...] = block_qp[:n_qkv]
    proj_o[...] = block_qp[n_qkv:]
    gain_o[...] = sums[0][packed_qp : packed_qp + 2, :lanes]
    for half in range(2):
        down_o[:, half * wide : (half + 1) * wide] = total_p(1, half)
    for copy in outs:
        copy.wait()
    for i in range(3):
        for k in range(reach):
            if k:
                far_w(i, k).wait_send()
                pair_w(i, k, lon).wait_send()
            near_w(i, k, lon).wait_send()
            pair_w(i, reach + k, lon).wait_send()
    for i in (0, 1):
        for k in range(reach):
            if k:
                far_p(i, k).wait_send()
            near_p(i, k).wait_send()
        for j in range(1, nlat):
            line_p(i, j).wait_send()
    for g in (0, 1):
        for i in range(3):
            halo(g, i).wait_send()
    for p in range(positions):
        for k in range(reach):
            if k:
                far_b(p, k).wait_send()
                far_t(p, k).wait_send()
            near_b(p, k).wait_send()
            near_t(p, k).wait_send()
        for j in range(1, nlat):
            row_t(p, j).wait_send()


def shards_fused(inputs, cotangent, qkv_weight, proj_weight, up_weight, down_weight, norm_gains, bias_table, type_of, region):
    levels, rows, cols, features = inputs.shape
    nlat, nlon = lax.axis_size("lat"), lax.axis_size("lon")
    level_windows = levels // WPL
    type_count, head_count, part = bias_table.shape
    positions, owners, reach, rows_n = level_windows, nlon, nlon // 2, nlat // 2
    n_up, n_qkv, n_proj = up_weight.shape[1], qkv_weight.shape[1], proj_weight.shape[1]
    gain_cols = norm_gains.shape[1]
    height = (n_qkv + n_proj + n_up) * 3 // 4 + SUB
    down, dw = down_weight.shape[1], down_weight.shape[0] // 2
    dma = pltpu.SemaphoreType.DMA
    vmem, hbm = pl.BlockSpec(memory_space=pltpu.VMEM), pl.BlockSpec(memory_space=pltpu.HBM)
    smem = pl.BlockSpec(memory_space=pltpu.SMEM)
    cell = (rows, cols, levels, features)
    per = WIN // owners
    blk = (-(-per * (head_count + 1) // 16) * 16, LANES)
    wide = (head_count + 1) * LANES
    a_shape, d_shape = (height, LANES), (down, dw)
    sizes = [(owners * n, features) for n in (n_qkv, n_proj, n_up)] + [(features, 2 * dw)]
    v = pltpu.VMEM
    lane_tiles = -(-features // LANES)
    scratch = [v((n_qkv, features), BF16), v((n_proj, features), BF16), v((features, n_up), BF16)]
    scratch += [v((down, 2 * dw), BF16), v((2, gain_cols), BF16), v((head_count, type_count, part), BF16)]
    scratch += [v((2,) + cell, BF16), v((owners, 2) + a_shape, BF16), v((owners, 2) + d_shape, BF16),
                v((positions, owners) + blk, BF16)]
    scratch += [v((lane_tiles, rows * cols * levels, LANES), F32)] + [v((positions, WIN, features), F32)] * 3
    scratch += [v((lane_tiles, WIN, LANES), F32), v((owners * blk[0], LANES), F32)]
    scratch += [v((head_count + 1, WIN, LANES), F32)]
    scratch += [v((WIN, wide), BF16)] * 2 + [v((wide, features), BF16)] * 2
    scratch += [v((per * SUB, LANES), F32)] * 2 + [v((positions,) + blk, F32)]
    scratch += [v(size, BF16) for size in sizes] + [v((2, features), F32)]
    scratch += [v(size, F32) for size in sizes] + [v((2, features), F32)]
    scratch += [v((2, owners) + a_shape, BF16), v((2, owners) + d_shape, BF16), v(cell, BF16)]
    scratch += [v((owners,) + s, BF16) for s in (a_shape, d_shape)] * 2
    scratch += [v((reach,) + s, BF16) for s in (a_shape, d_shape)] * 3
    scratch += [v((nlat,) + s, BF16) for s in (a_shape, d_shape)]
    scratch += [v((positions, owners) + blk, BF16)] + [v((positions, reach) + blk, BF16)] * 3
    scratch += [v((nlat, positions) + blk, BF16), v((nlat * positions * blk[0], LANES), F32)]
    scratch += [dma((6,)), dma((2,))] + [dma((2, 3))] * 2 + [dma((3, reach))] * 4 + [dma((3, nlon))] * 2
    scratch += [dma((positions, reach))] * 8 + [dma((positions, nlat))] * 2
    scratch += [dma((2,))] * 2 + [dma((2, reach))] * 4 + [dma((2, nlat))] * 2 + [dma((3,))] * 2
    outs = [(cell, BF16), ((n_qkv, features), F32), ((n_proj, features), F32), ((features, n_up), F32),
            ((down, 2 * dw), F32), ((2, gain_cols), F32), ((head_count, type_count, part), F32)]
    outs = [jax.ShapeDtypeStruct(*o) for o in outs]
    token_count = levels * rows * cols * nlat * nlon
    found = pl.pallas_call(
        functools.partial(fused_kernel, nlat, nlon, (n_up, n_qkv, n_proj), 1.0 / math.sqrt(token_count)),
        out_shape=outs,
        in_specs=[hbm] * 8 + [smem] * 2,
        out_specs=[vmem] * len(outs),
        scratch_shapes=scratch,
        compiler_params=pltpu.CompilerParams(
            collective_id=0, has_side_effects=True, vmem_limit_bytes=60 * 2**20
        ),
    )(
        inputs.transpose(1, 2, 0, 3), cotangent.transpose(1, 2, 0, 3),
        qkv_weight.T, proj_weight.T, up_weight, down_weight.T, norm_gains,
        bias_table.transpose(1, 0, 2), type_of, region,
    )
    grad, qkv, proj, up, down_g, gain, table = pl.pallas_call(
        finish_kernel,
        out_shape=outs,
        in_specs=[hbm] * len(outs),
        out_specs=[hbm] * len(outs),
        scratch_shapes=[v(o.shape, o.dtype) for o in outs] + [dma((2, len(outs)))],
        compiler_params=pltpu.CompilerParams(vmem_limit_bytes=60 * 2**20),
    )(*found)
    return grad.transpose(2, 0, 1, 3), qkv.T, proj.T, up, down_g.T, gain, table.transpose(1, 0, 2)


def shards(*args):
    inputs, bias_table = args[0], args[7]
    nlat, nlon = lax.axis_size("lat"), lax.axis_size("lon")
    levels, rows, cols, _ = inputs.shape
    heads = bias_table.shape[1]
    whole_rows = bias_table.shape[2] * nlon == WIN * WIN and nlon == SUB and WIN % nlon == 0
    one_window = rows == WLAT and cols == WLON and levels == SUB and nlat % 2 == 0
    ends_fit = WIN > LANES and (WIN - LANES) * heads <= LANES and heads < SUB
    n_qkv, n_proj, n_up, down = (args[i].shape[1] for i in (2, 3, 4, 5))
    tiled = n_qkv % SUB == 0 and (n_qkv + n_proj) % 32 == 0 and n_up % 32 == 0 and down % SUB == 0
    tiled = tiled and 2 * (inputs.shape[3] - LANES) == LANES
    if whole_rows and one_window and ends_fit and tiled:
        return shards_fused(*args)
    return shards_plain(*args)


def solution(mesh):
    return jax.shard_map(
        shards,
        mesh=mesh,
        in_specs=(
            P(None, "lat", "lon", None),
            P(None, "lat", "lon", None),
            P(None, "lon"),
            P(None, "lon"),
            P(None, "lon"),
            P(None, "lon"),
            P(None, "lon"),
            P(None, None, "lon"),
            P(),
            P(None, "lat"),
        ),
        out_specs=(
            P(None, "lat", "lon", None),
            P(None, "lon"),
            P(None, "lon"),
            P(None, "lon"),
            P(None, "lon"),
            P(None, "lon"),
            P(None, None, "lon"),
        ),
        check_vma=False,
    )
```

```python
import functools
import math

import jax
import jax.numpy as jnp
from jax import lax
from jax.experimental import pallas as pl
from jax.experimental.pallas import tpu as pltpu
from jax.sharding import PartitionSpec as P

WPL = 2
WLAT = 6
WLON = 12
WIN = 144
MESH = pl.DeviceIdType.MESH
F32 = jnp.float32
BF16 = jnp.bfloat16


def layer_norm(values):
    row_mean = jnp.mean(values, axis=-1, keepdims=True)
    centred = values - row_mean
    variance = jnp.mean(centred * centred, axis=-1, keepdims=True)
    inv_std = lax.rsqrt(variance + 1e-05)
    return (centred * inv_std, inv_std)


def norm_back(d_normed, normed, inv_std):
    return inv_std * (
        d_normed
        - jnp.mean(d_normed, axis=-1, keepdims=True)
        - normed * jnp.mean(d_normed * normed, axis=-1, keepdims=True)
    )


def gelu_pair(pre_act):
    cumul = 0.5 * (1.0 + lax.erf(pre_act * 0.7071067811865476))
    density = jnp.exp(-0.5 * pre_act * pre_act) * 0.3989422804014327
    return (pre_act * cumul, cumul + pre_act * density)


def position(nlat, nlon):
    lat, lon = lax.axis_index("lat"), lax.axis_index("lon")

    def at(dlat, dlon):
        return (lax.rem(lat + dlat + nlat, nlat), lax.rem(lon + dlon + nlon, nlon))

    core, side = lax.rem(lat, 2), lax.rem(lon, 2)
    twin = (lat + 1 - 2 * core, lon)
    across = (lat, lon + 1 - 2 * side)
    return lat, lon, at, core, twin, across


def greet(devices):
    barrier = pltpu.get_barrier_semaphore()
    for device in devices:
        pl.semaphore_signal(barrier, inc=1, device_id=device, device_id_type=MESH)
    pl.semaphore_wait(barrier, len(devices))


def peers(nlat, nlon, at, twin, across):
    steps = [(0, d) for d in range(2, nlon, 2)] + [(d, 0) for d in range(2, nlat, 2)]
    steps += [(1, 0), (-1, 0), (0, 1), (0, -1), (1, 1), (-1, -1)]
    return [twin, across] + [at(*step) for step in steps]


def send(src, dst, send_sem, recv_sem, device):
    copy = pltpu.make_async_remote_copy(
        src_ref=src, dst_ref=dst, send_sem=send_sem, recv_sem=recv_sem, device_id=device, device_id_type=MESH
    )
    copy.start()
    return copy


def gather_kernel(nlat, nlon, a, d, b, h_lat, h_lon, h_diag, a_all, d_all, b_all, r_lat, r_lon, r_diag,
                  zs, zr, xs, xr, ts, tr, hs, hr):
    lat, lon, at, core, twin, across = position(nlat, nlon)
    greet(peers(nlat, nlon, at, twin, across))
    reach = nlon // 2
    srcs = (a.at[core], d.at[core], b)

    def slots(owner):
        return (a_all.at[owner, core], d_all.at[owner, core], b_all.at[owner])

    far, near, shared, halo = {}, {}, [], []
    for k in range(1, reach):
        for i in range(3):
            far[i, k] = send(srcs[i], slots(lon)[i], zs.at[i, k], zr.at[i, k], at(0, 2 * k))
    for i in range(3):
        near[i, 0] = send(srcs[i], slots(lon)[i], xs.at[i, 0], xr.at[i, 0], across)
    for i, (src, dst, step) in enumerate(
        ((h_lat, r_lat, (-1, 0)), (h_lon, r_lon, (0, -1)), (h_diag, r_diag, (-1, -1)))
    ):
        halo.append(send(src, dst, hs.at[i], hr.at[i], at(*step)))
    a_all[lon] = a[...]
    d_all[lon] = d[...]
    b_all[lon] = b[...]
    for k in range(1, reach):
        owner = lax.rem(lon - 2 * k + nlon, nlon)
        for i in range(3):
            slot = slots(owner)[i]
            far[i, k].wait_recv()
            near[i, k] = send(slot, slot, xs.at[i, k], xr.at[i, k], across)
            if i < 2:
                shared.append(send(slot, slot, ts.at[i, k], tr.at[i, k], twin))
    for k in range(reach):
        owner = lax.rem(across[1] - 2 * k + nlon, nlon)
        for i in range(3):
            slot = slots(owner)[i]
            near[i, k].wait_recv()
            if i < 2:
                shared.append(send(slot, slot, ts.at[i, reach + k], tr.at[i, reach + k], twin))
    for copy in list(far.values()) + list(near.values()):
        copy.wait_send()
    for copy in halo + shared:
        copy.wait()


def reduce_kernel(nlat, nlon, scale, a, d, t, kron, h_lat, h_lon, h_diag, a_out, d_out, t_out, r_lat, r_lon, r_diag,
                  a_twin, d_twin, a_half, d_half, a_x, d_x, t_x, a_mid, d_mid, t_mid, a_z, d_z, t_z,
                  a_row, d_row, t_row, cs, cr, xs, xr, zs, zr, ls, lr, fs, fr, hs, hr):
    lat, lon, at, core, twin, across = position(nlat, nlon)
    greet(peers(nlat, nlon, at, twin, across))
    reach = nlon // 2
    near, far, rest = {}, {}, []
    order = list(range(1, reach)) + [0]
    pairs = [
        send(src.at[1 - core], dst, cs.at[i], cr.at[i], twin)
        for i, (src, dst) in enumerate(((a, a_twin), (d, d_twin)))
    ]

    def cross(i, src, dst):
        for k in order:
            owner = lax.rem(across[1] + 2 * k, nlon)
            near[i, k] = send(src.at[owner], dst.at[k], xs.at[i, k], xr.at[i, k], across)

    cross(2, t, t_x)
    for i, (src, dst, step) in enumerate(
        ((h_lat, r_lat, (1, 0)), (h_lon, r_lon, (0, 1)), (h_diag, r_diag, (1, 1)))
    ):
        rest.append(send(src, dst, hs.at[i], hr.at[i], at(*step)))
    for i, (own, got, half, dst) in enumerate(((a, a_twin, a_half, a_x), (d, d_twin, d_half, d_x))):
        pairs[i].wait()
        half[...] = (own[core].astype(F32) + got[...].astype(F32)).astype(BF16)
        cross(i, half, dst)
    streams = ((2, t, t_x, t_mid, t_z), (0, a_half, a_x, a_mid, a_z), (1, d_half, d_x, d_mid, d_z))
    for i, own, got, mid, dst in streams:
        for k in range(1, reach):
            owner = lax.rem(lon + 2 * k, nlon)
            near[i, k].wait_recv()
            mid[k] = (own[owner].astype(F32) + got[k].astype(F32)).astype(BF16)
            far[i, k] = send(mid.at[k], dst.at[k], zs.at[i, k], zr.at[i, k], at(0, 2 * k))
    rows = nlat // 2
    row = lax.div(lat, 2)

    def total_of(i, own, got, dst):
        near[i, 0].wait_recv()
        total = own[lon].astype(F32) + got[0].astype(F32)
        for k in range(1, reach):
            far[i, k].wait_recv()
            total = total + dst[k].astype(F32)
        return total.astype(BF16)

    t_row[lat] = total_of(2, t, t_x, t_z)
    rest.append(send(t_row.at[lat], t_row.at[lat], ls.at[2, 0], lr.at[2, 0], twin))
    t_far = [send(t_row.at[lat], t_row.at[lat], ls.at[2, j], lr.at[2, j], at(2 * j, 0)) for j in range(1, rows)]
    halves = []
    for i, own, got, dst, line in ((0, a_half, a_x, a_z, a_row), (1, d_half, d_x, d_z, d_row)):
        line[row] = total_of(i, own, got, dst)
        halves.append(
            [send(line.at[row], line.at[row], ls.at[i, j], lr.at[i, j], at(2 * j, 0)) for j in range(1, rows)]
        )
    for j in range(1, rows):
        slot = t_row.at[lax.rem(lat - 2 * j + nlat, nlat)]
        t_far[j - 1].wait_recv()
        rest.append(send(slot, slot, fs.at[2, j], fr.at[2, j], twin))
    for i, (line, out) in enumerate(((a_row, a_out), (d_row, d_out))):
        for copy in halves[i]:
            copy.wait_recv()
        total = line[0].astype(F32)
        for j in range(1, rows):
            total = total + line[j].astype(F32)
        out[core] = total * scale
        rest.append(send(out.at[core], out.at[core], fs.at[i, 0], fr.at[i, 0], twin))
    for copy in list(near.values()) + list(far.values()) + t_far + halves[0] + halves[1]:
        copy.wait_send()
    for copy in rest:
        copy.wait()
    total = jnp.zeros(t_out.shape, F32)
    for i in range(nlat):
        total = total + jnp.dot(kron[i], t_row[i], preferred_element_type=F32)
    t_out[...] = total


def comm_call(kernel, collective_id, outs, scratch, operands):
    vmem = pl.BlockSpec(memory_space=pltpu.VMEM)
    return pl.pallas_call(
        kernel,
        out_shape=[jax.ShapeDtypeStruct(*o) for o in outs],
        in_specs=[vmem] * len(operands),
        out_specs=[vmem] * len(outs),
        scratch_shapes=scratch,
        compiler_params=pltpu.CompilerParams(
            collective_id=collective_id, has_side_effects=True, vmem_limit_bytes=48 * 2**20
        ),
    )(*operands)


def to_windows(grid):
    p, l, c = grid.shape[:3]
    shaped = grid.reshape(p // WPL, WPL, l // WLAT, WLAT, c // WLON, WLON, grid.shape[-1])
    return shaped.transpose(4, 0, 2, 1, 3, 5, 6).reshape(-1, grid.shape[-1])


def from_windows(flat, p, l, c):
    shaped = flat.reshape(c // WLON, p // WPL, l // WLAT, WPL, WLAT, WLON, flat.shape[-1])
    return shaped.transpose(1, 3, 2, 4, 0, 5, 6).reshape(p, l, c, flat.shape[-1])


def by_t(x, w_t):
    return lax.dot_general(x, w_t, (((1,), (1,)), ((), ())), preferred_element_type=F32)


def outer(x, y):
    return lax.dot_general(x, y, (((0,), (0,)), ((), ())), preferred_element_type=F32)


def plain(x, y):
    return jnp.dot(x, y, preferred_element_type=F32)


def pick_kernel(types, table, out):
    positions = types.shape[0]
    rows = [table[types[i]].astype(F32) for i in range(positions)]
    out[...] = jnp.concatenate(rows, axis=0).astype(BF16)


def pick_rows(types, table):
    _, head_count, part = table.shape
    return pl.pallas_call(
        pick_kernel,
        out_shape=jax.ShapeDtypeStruct((types.shape[0] * head_count, part), BF16),
        in_specs=[pl.BlockSpec(memory_space=pltpu.SMEM), pl.BlockSpec(memory_space=pltpu.VMEM)],
        out_specs=pl.BlockSpec(memory_space=pltpu.VMEM),
    )(types, table)


def window_kernel(n_up, n_qkv, n_proj, cells, cots, a_all, d_all, bias, label_col, label_row,
                  d_cells, ga, gd, table,
                  probs_s, qkv_t, proj_t, up_t, down_t, gains, g_qkv, g_proj, g_up, g_down, g_gain):
    owners, height = a_all.shape[0], a_all.shape[2]

    def joined(half, start, count):
        rows = [a_all[j, half].astype(F32)[start : start + count] for j in range(owners)]
        return jnp.concatenate(rows, axis=0).astype(BF16)

    up_t[...] = joined(0, 0, n_up)
    qkv_t[...] = joined(1, 0, n_qkv)
    proj_t[...] = joined(1, n_qkv, n_proj)
    wide = d_all.shape[3]
    for i in range(2):
        rows = [d_all[j, i].astype(F32) for j in range(owners)]
        down_t[:, i * wide : (i + 1) * wide] = jnp.concatenate(rows, axis=0).astype(BF16)
    gain_sum = a_all[0, 0].astype(F32)[n_up : n_up + 2]
    for j in range(1, owners):
        gain_sum = gain_sum + a_all[j, 0].astype(F32)[n_up : n_up + 2]
    gains[...] = gain_sum
    positions, head_count = bias.shape[:2]
    windows, _, features = cells.shape
    head_size = features // head_count
    factor = 1.0 / math.sqrt(head_size)
    for total in (g_qkv, g_proj, g_up, g_down, g_gain):
        total[...] = jnp.zeros(total.shape, F32)
    if windows > positions:
        table[...] = jnp.zeros(table.shape, F32)

    def body(w, carry):
        p = lax.rem(w, positions)
        gain_one, gain_two = gains[0:1], gains[1:2]
        lane_head = lax.broadcasted_iota(jnp.int32, (1, features), 1) // head_size
        heads = [(lane_head == h).astype(BF16) for h in range(head_count)]
        normed_one, inv_one = layer_norm(cells[w].astype(F32))
        scaled_one = (normed_one * gain_one).astype(BF16)
        q, k, v = (
            by_t(scaled_one, qkv_t[i * features : (i + 1) * features]).astype(BF16) for i in range(3)
        )
        same = label_col[p] == label_row[p]
        attended = jnp.zeros((WIN, features), F32)
        for h, head in enumerate(heads):
            scores = by_t(q * head, k) * factor + bias[p, h].astype(F32)
            scores = jnp.where(same, scores, -jnp.inf)
            raised = jnp.exp(scores - jnp.max(scores, axis=-1, keepdims=True))
            probs = raised * (1.0 / jnp.sum(raised, axis=-1, keepdims=True))
            probs_s[h] = probs
            attended = attended + plain(probs.astype(BF16), v * head)
        attended = attended.astype(BF16)
        middle = cells[w].astype(F32) + by_t(attended, proj_t[...])
        normed_two, inv_two = layer_norm(middle)
        scaled_two = (normed_two * gain_two).astype(BF16)
        cot = cots[w]
        activated, slope = gelu_pair(by_t(scaled_two, up_t[...]))
        g_down[...] += outer(cot, activated.astype(BF16))
        d_hidden = (plain(cot, down_t[...]) * slope).astype(BF16)
        g_up[...] += outer(d_hidden, scaled_two)
        d_htwo = plain(d_hidden, up_t[...])
        g_gain[1:2] += jnp.sum(d_htwo * normed_two, axis=0, keepdims=True)
        d_middle = cot.astype(F32) + norm_back(d_htwo * gain_two, normed_two, inv_two)
        d_middle_b = d_middle.astype(BF16)
        g_proj[...] += outer(d_middle_b, attended)
        d_att = plain(d_middle_b, proj_t[...]).astype(BF16)
        d_q, d_k, d_v = (jnp.zeros((WIN, features), F32) for _ in range(3))
        for h, head in enumerate(heads):
            probs, d_att_h = probs_s[h], d_att * head
            d_prob = by_t(d_att_h, v)
            d_v = d_v + outer(probs.astype(BF16), d_att_h)
            d_score = probs * (d_prob - jnp.sum(probs * d_prob, axis=-1, keepdims=True))
            if windows > positions:
                table[p, h] += d_score
            else:
                table[p, h] = d_score.astype(table.dtype)
            d_score_b = d_score.astype(BF16)
            d_q = d_q + plain(d_score_b, k * head)
            d_k = d_k + outer(d_score_b, q * head)
        d_hone = jnp.zeros((WIN, features), F32)
        for i, part in enumerate((d_q * factor, d_k * factor, d_v)):
            part = part.astype(BF16)
            span = slice(i * features, (i + 1) * features)
            g_qkv[span] += outer(part, scaled_one)
            d_hone = d_hone + plain(part, qkv_t[span])
        g_gain[0:1] += jnp.sum(d_hone * normed_one, axis=0, keepdims=True)
        d_cells[w] = (d_middle + norm_back(d_hone * gain_one, normed_one, inv_one)).astype(BF16)
        return carry

    lax.fori_loop(0, windows, body, 0)
    features = cells.shape[2]
    down = d_all.shape[2]
    gain_rows = jnp.concatenate([g_gain[...], jnp.zeros((height - n_up - 2, features), F32)], axis=0)
    spare = height - n_qkv - n_proj
    for j in range(owners):
        ga[0, j] = jnp.concatenate([g_up[j * n_up : (j + 1) * n_up], gain_rows], axis=0).astype(BF16)
        rows = [g_qkv[j * n_qkv : (j + 1) * n_qkv], g_proj[j * n_proj : (j + 1) * n_proj]]
        rows += [jnp.zeros((spare, features), F32)] if spare else []
        ga[1, j] = jnp.concatenate(rows, axis=0).astype(BF16)
        for i in range(2):
            gd[i, j] = g_down[j * down : (j + 1) * down, i * wide : (i + 1) * wide].astype(BF16)


def block_grads(cells, cots, a_all, d_all, cuts, bias, labels):
    features = cells.shape[1]
    positions, head_count = bias.shape[:2]
    windows, owners, wide = cells.shape[0] // WIN, a_all.shape[0], d_all.shape[3] * 2
    vmem = pl.BlockSpec(memory_space=pltpu.VMEM)
    outs = [((windows, WIN, features), BF16)]
    outs += [((2, owners) + x.shape[2:], BF16) for x in (a_all, d_all)]
    outs += [(bias.shape, F32 if windows > positions else BF16)]
    n_up, n_qkv, n_proj = cuts
    sizes = [(owners * n, features) for n in (n_qkv, n_proj, n_up)] + [(features, wide)]
    d_cells, *grads = pl.pallas_call(
        functools.partial(window_kernel, *cuts),
        out_shape=[jax.ShapeDtypeStruct(*o) for o in outs],
        in_specs=[vmem] * 7,
        out_specs=[vmem] * len(outs),
        scratch_shapes=[pltpu.VMEM((head_count, WIN, WIN), F32)]
        + [pltpu.VMEM(size, BF16) for size in sizes] + [pltpu.VMEM((2, features), F32)]
        + [pltpu.VMEM(size, F32) for size in sizes] + [pltpu.VMEM((2, features), F32)],
        compiler_params=pltpu.CompilerParams(vmem_limit_bytes=48 * 2**20),
    )(
        cells.reshape(windows, WIN, features), cots.reshape(windows, WIN, features),
        a_all, d_all, bias, labels[:, :, None], labels[:, None, :],
    )
    return (d_cells.reshape(cells.shape), *grads)


def shards_plain(inputs, cotangent, qkv_weight, proj_weight, up_weight, down_weight, norm_gains, bias_table, type_of, region):
    levels, rows, cols, features = inputs.shape
    nlat, nlon = lax.axis_size("lat"), lax.axis_size("lon")
    level_windows, row_windows = levels // WPL, rows // WLAT
    type_count, head_count, part = bias_table.shape
    positions = level_windows * row_windows
    lat_index = lax.axis_index("lat")
    row_half, col_half, level_shift = WLAT // 2, WLON // 2, WPL // 2
    all_types = type_of.reshape(level_windows, nlat, row_windows).transpose(1, 0, 2).reshape(nlat, positions)
    types = lax.dynamic_index_in_dim(all_types, lat_index, 0, keepdims=False)
    n_up, n_qkv, n_proj = up_weight.shape[1], qkv_weight.shape[1], proj_weight.shape[1]
    gain_cols, height = norm_gains.shape[1], -(-max(n_up + 2, n_qkv + n_proj) // 8) * 8
    gain_spot = lax.axis_index("lon") * gain_cols
    own_lane = jnp.arange(features, dtype=jnp.int32) // gain_cols == lax.axis_index("lon")
    gain_rows = jnp.where(own_lane, jnp.tile(norm_gains, (1, nlon)), jnp.zeros((), BF16))
    gain_rows = jnp.pad(gain_rows, ((0, height - n_up - 2), (0, 0)))
    a_part = jnp.stack(
        [
            jnp.concatenate([up_weight.T, gain_rows]),
            jnp.pad(
                jnp.concatenate([qkv_weight.T, proj_weight.T]), ((0, height - n_qkv - n_proj), (0, 0))
            ),
        ]
    )
    d_part = down_weight.reshape(2, -1, down_weight.shape[1]).transpose(0, 2, 1)
    b_part = pick_rows(types, bias_table)
    both = jnp.roll(jnp.stack([inputs, cotangent]), -level_shift, axis=1)
    rim_lat = both[:, :, :row_half, col_half:]
    rim_lon = both[:, :, row_half:, :col_half]
    rim_diag = both[:, :, :row_half, :col_half]
    flat = [r.reshape(-1, features) for r in (rim_lat, rim_lon, rim_diag)]
    dma = pltpu.SemaphoreType.DMA
    a_all, d_all, b_all, r_lat, r_lon, r_diag = comm_call(
        functools.partial(gather_kernel, nlat, nlon),
        0,
        [((nlon,) + x.shape, BF16) for x in (a_part, d_part, b_part)] + [(x.shape, BF16) for x in flat],
        [dma((3, nlon // 2))] * 4 + [dma((2, nlon))] * 2 + [dma((3,))] * 2,
        (a_part, d_part, b_part, *flat),
    )
    bias = b_all.transpose(1, 0, 2).reshape(positions, head_count, WIN, WIN)
    top = jnp.concatenate([both[:, :, row_half:, col_half:], r_lon.reshape(rim_lon.shape)], axis=3)
    bottom = jnp.concatenate([r_lat.reshape(rim_lat.shape), r_diag.reshape(rim_diag.shape)], axis=3)
    shifted = jnp.concatenate([top, bottom], axis=2)
    labels = region.reshape(level_windows, WPL, row_windows, WLAT).transpose(0, 2, 1, 3)
    labels = jnp.broadcast_to(labels[..., None], labels.shape + (WLON,)).reshape(positions, WIN)
    d_cells, ga, gd, table = block_grads(
        to_windows(shifted[0]), to_windows(shifted[1]), a_all, d_all, (n_up, n_qkv, n_proj), bias, labels
    )
    gt = table.astype(BF16).reshape(positions * head_count, nlon, part).transpose(1, 0, 2)
    onehot = (all_types[:, None, :] == jnp.arange(type_count, dtype=jnp.int32)[None, :, None]).astype(BF16)
    kron = jnp.einsum("lyp,gh->lygph", onehot, jnp.eye(head_count, dtype=BF16)).reshape(
        nlat, type_count * head_count, positions * head_count
    )
    back = from_windows(d_cells, levels, rows, cols)
    out_lat = back[:, rows - row_half :, : cols - col_half]
    out_lon = back[:, : rows - row_half, cols - col_half :]
    out_diag = back[:, rows - row_half :, cols - col_half :]
    flat = [r.reshape(-1, features) for r in (out_lat, out_lon, out_diag)]
    shard_shapes = (ga.shape[2:], gd.shape[2:], gt.shape[1:])
    token_count = levels * rows * cols * nlat * nlon
    a_sum, d_sum, t_sum, r_lat, r_lon, r_diag = comm_call(
        functools.partial(reduce_kernel, nlat, nlon, 1.0 / math.sqrt(token_count)),
        1,
        [((2,) + ga.shape[2:], F32), ((2,) + gd.shape[2:], F32), ((type_count * head_count, part), F32)]
        + [(x.shape, BF16) for x in flat],
        [pltpu.VMEM(x.shape[1:], BF16) for x in (ga, gd)] * 2
        + [pltpu.VMEM((nlon // 2,) + shape, BF16) for shape in shard_shapes] * 3
        + [pltpu.VMEM((nlat // 2,) + shape, BF16) for shape in shard_shapes[:2]]
        + [pltpu.VMEM((nlat,) + shard_shapes[2], BF16)]
        + [dma((2,))] * 2 + [dma((3, nlon // 2))] * 4 + [dma((3, nlat // 2))] * 4 + [dma((3,))] * 2,
        (ga, gd, gt, kron, *flat),
    )
    own = back[:, : rows - row_half, : cols - col_half]
    top = jnp.concatenate([r_diag.reshape(out_diag.shape), r_lat.reshape(out_lat.shape)], axis=2)
    bottom = jnp.concatenate([r_lon.reshape(out_lon.shape), own], axis=2)
    grad_input = jnp.roll(jnp.concatenate([top, bottom], axis=1), level_shift, axis=0)
    return (
        grad_input,
        a_sum[1, :n_qkv].T,
        a_sum[1, n_qkv : n_qkv + n_proj].T,
        a_sum[0, :n_up].T,
        d_sum.transpose(0, 2, 1).reshape(down_weight.shape),
        lax.dynamic_slice(a_sum[0, n_up : n_up + 2], (jnp.int32(0), gain_spot), (2, gain_cols)),
        t_sum.reshape(type_count, head_count, part),
    )


LANES = 128
SUB = 8


def rc(src, dst, send_sem, recv_sem, device):
    return pltpu.make_async_remote_copy(
        src_ref=src, dst_ref=dst, send_sem=send_sem, recv_sem=recv_sem, device_id=device, device_id_type=MESH
    )


def all_peers(nlat, nlon, at, across):
    steps = [(0, d) for d in range(2, nlon, 2)] + [(d, 0) for d in range(1, nlat)]
    steps += [(0, 1), (0, -1), (1, 1), (-1, -1)]
    return [across] + [at(*step) for step in steps]


def finish_kernel(*refs):
    count = (len(refs) - 1) // 3
    srcs, dsts, held, sems = refs[:count], refs[count : 2 * count], refs[2 * count : -1], refs[-1]
    loads = [pltpu.make_async_copy(srcs[i], held[i], sems.at[0, i]) for i in range(count)]
    stores = [pltpu.make_async_copy(held[i], dsts[i], sems.at[1, i]) for i in range(count)]
    for copy in loads:
        copy.start()
    for load, copy in zip(loads, stores):
        load.wait()
        copy.start()
    for copy in stores:
        copy.wait()


def fused_kernel(nlat, nlon, cuts, scale, x_in, c_in, qkv_in, proj_in, up_in, down_in, gain_in, tab_in, types, region,
                 out, qkv_o, proj_o, up_o, down_o, gain_o, t_out,
                 qkv_v, proj_v, up_v, down_v, gain_v, tab,
                 own_v, tail_v, grid, a_all, d_all, b_all,
                 wide_s, cells_s, cots_s, dcell_s, perm_s, asm_s, score_s, prob_b, ds_b, kexp_s, vexp_s,
                 pick_m, pick_t, pick_u,
                 qkv_t, proj_t, up_t, down_t, gains, g_qkv, g_proj, g_up, g_down, g_gain,
                 ga, gd, obuf, a_twin, d_twin, a_half, d_half, a_x, d_x, a_mid, d_mid, a_z, d_z, a_row, d_row,
                 t_w, t_x, t_mid, t_z, t_row, t_val,
                 in_s, own_s, hs, hr, wzs, wzr, wxs, wxr, wts, wtr, bzs, bzr, bxs, bxr,
                 txs, txr, tzs, tzr, tls, tlr,
                 pcs, pcr, pxs, pxr, pzs, pzr, pls, plr, ohs, ohr):
    n_up, n_qkv, n_proj = cuts
    lat, lon, at, core, twin, across = position(nlat, nlon)
    rows_c, cols_c, levels, features = x_in.shape
    half_r, half_c = rows_c // 2, cols_c // 2
    head_count = tab.shape[0]
    type_count = tab.shape[1]
    positions = types.shape[0]
    owners, height, wide = nlon, a_all.shape[2], d_all.shape[3]
    lines_qp, lines_up = (n_qkv + n_proj) // 2, n_up // 2
    packed_qp, packed_up = lines_qp * 3 // 2, lines_up * 3 // 2
    side = features - LANES
    beats = head_count + 1
    span_b = b_all.shape[2]
    reach, rows_n = nlon // 2, nlat // 2
    head_size = features // head_count
    per = WIN // owners
    spare = WIN - LANES
    factor = 1.0 / math.sqrt(head_size)
    slab = WIN // WPL

    loads = [
        pltpu.make_async_copy(src, dst, in_s.at[i])
        for i, (src, dst) in enumerate(
            ((qkv_in, qkv_v), (proj_in, proj_v), (up_in, up_v), (gain_in, gain_v), (tab_in, tab), (down_in, down_v))
        )
    ]
    for copy in loads:
        copy.start()

    tiles = [(t, t * LANES, min(LANES, features - t * LANES)) for t in range(-(-features // LANES))]

    def fill(ref, value):
        for t, start, count in tiles:
            ref[t, :, :count] = value[:, start : start + count]

    def whole(ref):
        return jnp.concatenate([ref[t][:, :count] for t, _, count in tiles], axis=1)

    def strided(ref, start, size, stride):
        return jnp.concatenate(
            [ref.at[t][pl.ds(start, size, stride=stride), :][:, :count] for t, _, count in tiles], axis=1
        )

    def store_strided(ref, start, size, stride, value):
        for t, first, count in tiles:
            piece = value[:, first : first + count]
            if count < LANES:
                piece = jnp.concatenate([piece, jnp.zeros((size, LANES - count), F32)], axis=1)
            ref.at[t][pl.ds(start, size, stride=stride), :] = piece

    def pack(block):
        half = block.shape[0] // 2
        return jnp.concatenate(
            [block[:, :LANES], jnp.concatenate([block[:half, LANES:], block[half:, LANES:]], axis=1)], axis=0
        )

    def unpack(block):
        count = block.shape[0] * 2 // 3
        tail = jnp.concatenate([block[count:, :side], block[count:, side:]], axis=0)
        return jnp.concatenate([block[:count], tail], axis=1)

    lo_r, hi_r = pl.ds(0, half_r), pl.ds(half_r, rows_c - half_r)
    lo_c, hi_c = pl.ds(0, half_c), pl.ds(half_c, cols_c - half_c)
    end_r, end_c = pl.ds(rows_c - half_r, half_r), pl.ds(cols_c - half_c, half_c)
    first_r, first_c = pl.ds(0, rows_c - half_r), pl.ds(0, cols_c - half_c)

    main = pl.ds(0, LANES)

    def halo(g, i):
        src = tail_v if g == 2 else (x_in, c_in)[g].at[:, :, :, main]
        dst = grid.at[g]
        if i == 0:
            return rc(src.at[lo_r, hi_c], dst.at[end_r, first_c], hs.at[g, i], hr.at[g, i], at(-1, 0))
        if i == 1:
            return rc(src.at[hi_r, lo_c], dst.at[first_r, end_c], hs.at[g, i], hr.at[g, i], at(0, -1))
        return rc(src.at[lo_r, lo_c], dst.at[end_r, end_c], hs.at[g, i], hr.at[g, i], at(-1, -1))

    def own(g):
        return pltpu.make_async_copy((x_in, c_in)[g], own_v.at[g], own_s.at[g])

    for g in (0, 1):
        own(g).start()

    top = packed_qp + SUB

    def w_slot(i, owner):
        if i == 2:
            return d_all.at[owner, core]
        return a_all.at[owner, core].at[pl.ds(0, top) if i == 0 else pl.ds(top, packed_up)]

    def far_w(i, k):
        return rc(w_slot(i, lon), w_slot(i, lon), wzs.at[i, k], wzr.at[i, k], at(0, 2 * k))

    def near_w(i, k, owner):
        return rc(w_slot(i, owner), w_slot(i, owner), wxs.at[i, k], wxr.at[i, k], across)

    def pair_w(i, k, owner):
        return rc(w_slot(i, owner), w_slot(i, owner), wts.at[i, k], wtr.at[i, k], twin)

    def send_w(i):
        for k in range(1, reach):
            far_w(i, k).start()
        near_w(i, 0, lon).start()

    def pass_far(i):
        for k in range(1, reach):
            owner = lax.rem(lon - 2 * k + nlon, nlon)
            far_w(i, k).wait_recv()
            near_w(i, k, owner).start()
            pair_w(i, k, owner).start()

    def pass_near(i):
        for k in range(reach):
            owner = lax.rem(across[1] - 2 * k + nlon, nlon)
            near_w(i, k, owner).wait_recv()
            pair_w(i, reach + k, owner).start()

    def end_pair(i):
        for k in range(1, 2 * reach):
            pair_w(i, k, lon).wait_recv()

    greet(all_peers(nlat, nlon, at, across))
    for i in range(3):
        halo(0, i).start()
    for copy in loads[:4]:
        copy.wait()
    both = jnp.concatenate([qkv_v[...].astype(F32), proj_v[...].astype(F32)], axis=0)
    first = up_v[...].astype(F32).T
    gain_v32 = gain_v[...].astype(F32)
    gain_rows = jnp.concatenate([gain_v32, jnp.zeros((2, LANES - gain_v32.shape[1]), F32)], axis=1)
    gain_rows = jnp.concatenate([gain_rows, jnp.zeros((SUB - 2, LANES), F32)], axis=0)
    for i in range(2):
        a_all[lon, i] = jnp.concatenate(
            [
                pack(both[i * lines_qp : (i + 1) * lines_qp]),
                gain_rows,
                pack(first[i * lines_up : (i + 1) * lines_up]),
            ],
            axis=0,
        ).astype(BF16)
    send_w(0)
    for g in (0, 1):
        own(g).wait()
        grid[g, first_r, first_c] = own_v[g, hi_r, hi_c, :, :LANES]
    tails = [own_v[g].astype(F32).reshape(-1, features)[:, LANES:] for g in (0, 1)]
    tail_v[...] = jnp.concatenate(tails, axis=1).reshape(tail_v.shape).astype(BF16)
    grid[2, first_r, first_c] = tail_v[hi_r, hi_c]
    for i in range(3):
        halo(2, i).start()
    loads[4].wait()

    rows_i = lax.broadcasted_iota(jnp.int32, (SUB, type_count), 0)
    want = jnp.full((SUB, type_count), -1, jnp.int32)
    for i in range(positions):
        want = jnp.where(rows_i == i, types[i, lat], want)
    onehot = (lax.broadcasted_iota(jnp.int32, (SUB, type_count), 1) == want).astype(F32).astype(BF16)
    tails = [jnp.zeros((per, LANES), F32) for _ in range(positions)]
    for h in range(head_count):
        val = jnp.dot(onehot, tab[h], preferred_element_type=F32)
        for r in range(per):
            pick_m[r * SUB : (r + 1) * SUB] = val[:, r * WIN : r * WIN + LANES]
            end = val[:, r * WIN + LANES : (r + 1) * WIN]
            pick_t[r * SUB : (r + 1) * SUB] = jnp.concatenate([end, jnp.zeros((SUB, LANES - spare), F32)], axis=1)
        for i in range(positions):
            pick_u[i, pl.ds(h, per, stride=beats), :] = pick_m[pl.ds(i, per, stride=SUB), :]
            piece = pick_t[pl.ds(i, per, stride=SUB), :]
            tails[i] = tails[i] + (pltpu.roll(piece, h * spare, 1) if h else piece)
    for i in range(positions):
        pick_u[i, pl.ds(head_count, per, stride=beats), :] = tails[i]
        pick_u[i, per * beats :, :] = jnp.zeros((span_b - per * beats, LANES), F32)

    def far_b(p, k):
        return rc(b_all.at[p, lon], b_all.at[p, lon], bzs.at[p, k], bzr.at[p, k], at(0, 2 * k))

    def relay_b(p):
        rc(b_all.at[p, lon], b_all.at[p, lon], bxs.at[p, 0], bxr.at[p, 0], across).start()
        for k in range(1, reach):
            far_b(p, k).wait_recv()
            slot = b_all.at[p, lax.rem(lon - 2 * k + nlon, nlon)]
            rc(slot, slot, bxs.at[p, k], bxr.at[p, k], across).start()

    def near_b(p, k):
        slot = b_all.at[p, lon]
        return rc(slot, slot, bxs.at[p, k], bxr.at[p, k], across)

    for i in range(positions):
        b_all[i, lon] = pick_u[i].astype(BF16)

    def send_b(p):
        for k in range(1, reach):
            far_b(p, k).start()

    send_b(0)
    loads[5].wait()
    for i in range(2):
        d_all[lon, i] = down_v[:, i * wide : (i + 1) * wide]
    send_w(1)
    send_w(2)
    for i in range(3):
        halo(1, i).start()
    for i in range(1, positions):
        send_b(i)

    def windows_of(g, store):
        for i in range(3):
            halo(g, i).wait_recv()
            if g == 0:
                halo(2, i).wait_recv()
        wide_s[0] = grid[g].astype(F32).reshape(rows_c * cols_c * levels, LANES)
        ends = grid[2].astype(F32).reshape(rows_c * cols_c * levels, LANES)
        wide_s[1, :, :side] = ends[:, g * side : (g + 1) * side]
        for i in range(positions):
            for j in range(WPL):
                level = (WPL * i + j + WPL // 2) % levels
                store[i, j * slab : (j + 1) * slab] = strided(wide_s, level, slab, levels)

    for total in (g_qkv, g_proj, g_up, g_down, g_gain):
        total[...] = jnp.zeros(total.shape, F32)
    asm_s[...] = jnp.zeros(asm_s.shape, F32)
    pass_far(0)
    relay_b(0)
    windows_of(0, cells_s)
    pass_near(0)
    pass_far(1)
    pass_far(2)
    end_pair(0)
    for j in range(owners):
        rows = [unpack(a_all[j, i, :packed_qp].astype(F32)) for i in range(2)]
        rows = jnp.concatenate(rows, axis=0).astype(BF16)
        qkv_t[j * n_qkv : (j + 1) * n_qkv] = rows[:n_qkv]
        proj_t[j * n_proj : (j + 1) * n_proj] = rows[n_qkv:]
    lanes = features // owners
    gains[...] = jnp.concatenate(
        [a_all[j, 0, packed_qp:top].astype(F32)[:2, :lanes] for j in range(owners)], axis=1
    )

    def late_weights():
        pass_near(1)
        pass_near(2)
        windows_of(1, cots_s)
        end_pair(1)
        end_pair(2)
        for j in range(owners):
            rows = [unpack(a_all[j, i, top:].astype(F32)) for i in range(2)]
            up_t[j * n_up : (j + 1) * n_up] = jnp.concatenate(rows, axis=0).astype(BF16)
        for i in range(2):
            rows = [d_all[j, i].astype(F32) for j in range(owners)]
            down_t[:, i * wide : (i + 1) * wide] = jnp.concatenate(rows, axis=0).astype(BF16)

    def near_t(p, k):
        owner = lax.rem(across[1] + 2 * k, nlon)
        return rc(t_w.at[p, owner], t_x.at[p, k], txs.at[p, k], txr.at[p, k], across)

    def far_t(p, k):
        return rc(t_mid.at[p, k], t_z.at[p, k], tzs.at[p, k], tzr.at[p, k], at(0, 2 * k))

    order = list(range(1, reach)) + [0]

    def stage_one(p):
        for k in order:
            near_t(p, k).start()

    def stage_two(p):
        for k in range(1, reach):
            owner = lax.rem(lon + 2 * k, nlon)
            near_t(p, k).wait_recv()
            t_mid[p, k] = (t_w[p, owner].astype(F32) + t_x[p, k].astype(F32)).astype(BF16)
            far_t(p, k).start()

    def row_t(p, j):
        slot = t_row.at[lat, p]
        return rc(slot, slot, tls.at[p, j], tlr.at[p, j], at(j, 0))

    def stage_three(p):
        near_t(p, 0).wait_recv()
        total = t_w[p, lon].astype(F32) + t_x[p, 0].astype(F32)
        for k in range(1, reach):
            far_t(p, k).wait_recv()
            total = total + t_z[p, k].astype(F32)
        t_row[lat, p] = total.astype(BF16)
        for j in range(1, nlat):
            row_t(p, j).start()

    lane_head = lax.broadcasted_iota(jnp.int32, (1, features), 1) // head_size
    seg = lax.broadcasted_iota(jnp.int32, (1, LANES), 1) // spare

    def to_perm(value):
        fill(perm_s, value)
        return jnp.concatenate([strided(perm_s, r, SUB, per) for r in range(per)], axis=0)

    def from_perm(value):
        for r in range(per):
            store_strided(perm_s, r, SUB, per, value[r * SUB : (r + 1) * SUB])
        return whole(perm_s)

    def expand(dst, rows):
        low = rows[:LANES]
        high = rows[LANES:]
        ends = []
        for h in range(head_count):
            mine = lane_head == h
            dst[h * LANES : (h + 1) * LANES] = jnp.where(mine, low, 0.0).astype(BF16)
            ends.append(jnp.where(mine, high, 0.0))
        ends.append(jnp.zeros((LANES - head_count * spare, features), F32))
        dst[head_count * LANES :] = jnp.concatenate(ends, axis=0).astype(BF16)

    def collapse(big):
        low = big[:LANES]
        start = head_count * LANES
        high = big[start : start + spare]
        for h in range(1, head_count):
            mine = lane_head == h
            low = jnp.where(mine, big[h * LANES : (h + 1) * LANES], low)
            high = jnp.where(mine, big[start + h * spare : start + (h + 1) * spare], high)
        return jnp.concatenate([low, high], axis=0)

    def block(h):
        return slice(h * LANES, (h + 1) * LANES)

    token_k = lax.broadcasted_iota(jnp.int32, (1, LANES), 1)
    token_end = LANES + token_k - spare * seg
    place_q = lax.broadcasted_iota(jnp.int32, (WIN, 1), 0)
    turn_q = place_q >> (SUB.bit_length() - 1)
    token_q = per * (place_q - SUB * turn_q) + turn_q
    cells_r = rows_c * WPL

    def label_of(p, token):
        label = jnp.full(token.shape, region[WPL * p, 0], jnp.int32)
        for g in range(1, cells_r):
            label = jnp.where(token >= cols_c * g, region[WPL * p + g // rows_c, g % rows_c], label)
        return label

    def body(p, carry):
        gain_one, gain_two = gains[0:1], gains[1:2]
        normed_one, inv_one = layer_norm(cells_s[p])
        scaled_one = (normed_one * gain_one).astype(BF16)
        q, k, v = (by_t(scaled_one, qkv_t[i * features : (i + 1) * features]) for i in range(3))
        qp = to_perm(q).astype(BF16)
        expand(kexp_s, k)
        expand(vexp_s, v)
        for j in range(reach):
            near_b(p, j).wait_recv()
        for j in range(owners):
            asm_s[j * span_b : (j + 1) * span_b] = b_all[p, j].astype(F32)
        mine_q = label_of(p, token_q)
        same = mine_q == label_of(p, token_k)
        same_end = mine_q == jnp.where(seg < head_count, label_of(p, token_end), -1)

        def bias_of(h):
            return jnp.concatenate([asm_s[pl.ds(r * beats + h, SUB, stride=span_b), :] for r in range(per)], axis=0)

        def raw(h, keep):
            scores = by_t(qp, kexp_s[block(h)]) * factor + bias_of(h)
            return jnp.where(keep, scores, -jnp.inf)

        last = head_count
        s_end = raw(last, same_end)
        peak_end = jnp.zeros((WIN, LANES), F32)
        for h in range(head_count):
            mine = seg == h
            s = raw(h, same)
            peak = jnp.max(jnp.maximum(s, jnp.where(mine, s_end, -jnp.inf)), axis=-1, keepdims=True)
            score_s[h] = jnp.exp(s - peak)
            peak_end = jnp.where(mine, peak, peak_end)
        e_end = jnp.exp(s_end - peak_end)
        inv_end = jnp.zeros((WIN, LANES), F32)
        for h in range(head_count):
            mine = seg == h
            e = score_s[h]
            inv = 1.0 / jnp.sum(e + jnp.where(mine, e_end, 0.0), axis=-1, keepdims=True)
            probs = e * inv
            score_s[h] = probs
            prob_b[:, block(h)] = probs.astype(BF16)
            inv_end = jnp.where(mine, inv, inv_end)
        p_end = e_end * inv_end
        score_s[last] = p_end
        prob_b[:, block(last)] = p_end.astype(BF16)
        attended = from_perm(plain(prob_b[...], vexp_s[...])).astype(BF16)

        @pl.when(p == 0)
        def _():
            late_weights()
            if positions > 1:
                relay_b(1)

        middle = cells_s[p] + by_t(attended, proj_t[...])
        normed_two, inv_two = layer_norm(middle)
        scaled_two = (normed_two * gain_two).astype(BF16)
        cot = cots_s[p].astype(BF16)
        activated, slope = gelu_pair(by_t(scaled_two, up_t[...]))
        g_down[...] += outer(cot, activated.astype(BF16))
        d_hidden = (plain(cot, down_t[...]) * slope).astype(BF16)
        g_up[...] += outer(d_hidden, scaled_two)
        d_htwo = plain(d_hidden, up_t[...])
        g_gain[1:2] += jnp.sum(d_htwo * normed_two, axis=0, keepdims=True)
        d_middle = cots_s[p] + norm_back(d_htwo * gain_two, normed_two, inv_two)
        d_middle_b = d_middle.astype(BF16)
        g_proj[...] += outer(d_middle_b, attended)
        dap = to_perm(plain(d_middle_b, proj_t[...])).astype(BF16)

        p_end = score_s[last]
        dp_end = by_t(dap, vexp_s[block(last)])
        mix_end = p_end * dp_end
        dot_end = jnp.zeros((WIN, LANES), F32)

        def put(h, ds):
            ds_b[:, block(h)] = ds.astype(BF16)
            for r in range(per):
                asm_s[pl.ds(r * beats + h, SUB, stride=span_b), :] = ds[r * SUB : (r + 1) * SUB]

        for h in range(head_count):
            mine = seg == h
            probs = score_s[h]
            dp = by_t(dap, vexp_s[block(h)])
            dot = jnp.sum(probs * dp + jnp.where(mine, mix_end, 0.0), axis=-1, keepdims=True)
            dot_end = jnp.where(mine, dot, dot_end)
            put(h, probs * (dp - dot))
        put(last, p_end * (dp_end - dot_end))
        for j in range(owners):
            t_w[p, j] = asm_s[j * span_b : (j + 1) * span_b].astype(BF16)
        stage_one(p)
        d_q = from_perm(plain(ds_b[...], kexp_s[...]))
        d_k = collapse(outer(ds_b[...], qp))
        d_v = collapse(outer(prob_b[...], dap))
        d_hone = jnp.zeros((WIN, features), F32)
        for i, part in enumerate((d_q * factor, d_k * factor, d_v)):
            part = part.astype(BF16)
            span = slice(i * features, (i + 1) * features)
            g_qkv[span] += outer(part, scaled_one)
            d_hone = d_hone + plain(part, qkv_t[span])
        g_gain[0:1] += jnp.sum(d_hone * normed_one, axis=0, keepdims=True)
        dcell_s[p] = d_middle + norm_back(d_hone * gain_one, normed_one, inv_one)

        @pl.when(p + 2 < positions)
        def _():
            relay_b(p + 2)

        @pl.when(p >= 1)
        def _():
            stage_two(p - 1)

        @pl.when(p >= 2)
        def _():
            stage_three(p - 2)

        return carry

    lax.fori_loop(0, positions, body, 0)

    down = d_all.shape[2]
    no_gain = jnp.zeros((SUB, LANES), F32)
    for j in range(owners):
        block_qp = jnp.concatenate(
            [g_qkv[j * n_qkv : (j + 1) * n_qkv], g_proj[j * n_proj : (j + 1) * n_proj]], axis=0
        )
        block_up = g_up[j * n_up : (j + 1) * n_up]
        own_gain = jnp.concatenate([g_gain[:, j * lanes : (j + 1) * lanes], jnp.zeros((2, LANES - lanes), F32)], axis=1)
        own_gain = jnp.concatenate([own_gain, jnp.zeros((SUB - 2, LANES), F32)], axis=0)
        for i in range(2):
            ga[i, j] = jnp.concatenate(
                [
                    pack(block_qp[i * lines_qp : (i + 1) * lines_qp]),
                    no_gain if i else own_gain,
                    pack(block_up[i * lines_up : (i + 1) * lines_up]),
                ],
                axis=0,
            ).astype(BF16)
            gd[i, j] = g_down[j * down : (j + 1) * down, i * wide : (i + 1) * wide].astype(BF16)
    pairs = [
        rc(src.at[1 - core], dst, pcs.at[i], pcr.at[i], twin)
        for i, (src, dst) in enumerate(((ga, a_twin), (gd, d_twin)))
    ]
    for copy in pairs:
        copy.start()
    for i in range(positions):
        for j in range(WPL):
            level = (WPL * i + j + WPL // 2) % levels
            store_strided(wide_s, level, slab, levels, dcell_s[i, j * slab : (j + 1) * slab])
    obuf[...] = whole(wide_s).reshape(obuf.shape).astype(BF16)
    outs = [
        rc(obuf.at[end_r, first_c], out.at[lo_r, hi_c], ohs.at[0], ohr.at[0], at(1, 0)),
        rc(obuf.at[first_r, end_c], out.at[hi_r, lo_c], ohs.at[1], ohr.at[1], at(0, 1)),
        rc(obuf.at[end_r, end_c], out.at[lo_r, lo_c], ohs.at[2], ohr.at[2], at(1, 1)),
    ]
    out[hi_r, hi_c] = obuf[first_r, first_c]
    halves = (a_half, d_half)
    p_x, p_mid, p_z = (a_x, d_x), (a_mid, d_mid), (a_z, d_z)

    def near_p(i, k):
        owner = lax.rem(across[1] + 2 * k, nlon)
        return rc(halves[i].at[owner], p_x[i].at[k], pxs.at[i, k], pxr.at[i, k], across)

    def far_p(i, k):
        return rc(p_mid[i].at[k], p_z[i].at[k], pzs.at[i, k], pzr.at[i, k], at(0, 2 * k))

    for i, (mine, got) in enumerate(((ga, a_twin), (gd, d_twin))):
        pairs[i].wait()
        halves[i][...] = (mine[core].astype(F32) + got[...].astype(F32)).astype(BF16)
        for k in order:
            near_p(i, k).start()
    for copy in outs:
        copy.start()
    for p in range(max(positions - 1, 0), positions):
        stage_two(p)
    for p in range(max(positions - 2, 0), positions - 1):
        stage_three(p)
    for i in (0, 1):
        for k in range(1, reach):
            owner = lax.rem(lon + 2 * k, nlon)
            near_p(i, k).wait_recv()
            p_mid[i][k] = (halves[i][owner].astype(F32) + p_x[i][k].astype(F32)).astype(BF16)
            far_p(i, k).start()
    stage_three(positions - 1)
    lines = (a_row, d_row)

    def line_p(i, j):
        slot = lines[i].at[lat]
        return rc(slot, slot, pls.at[i, j], plr.at[i, j], at(j, 0))

    for i in (0, 1):
        near_p(i, 0).wait_recv()
        total = halves[i][lon].astype(F32) + p_x[i][0].astype(F32)
        for k in range(1, reach):
            far_p(i, k).wait_recv()
            total = total + p_z[i][k].astype(F32)
        lines[i][lat] = total.astype(BF16)
        for j in range(1, nlat):
            line_p(i, j).start()
    for p in range(positions):
        for j in range(1, nlat):
            row_t(p, j).wait_recv()
    spots = nlat * positions
    for i in range(nlat):
        for p in range(positions):
            t_val[(i * positions + p) * span_b : (i * positions + p + 1) * span_b] = t_row[i, p].astype(F32)
    cols_i = lax.broadcasted_iota(jnp.int32, (type_count, spots), 1)
    want = jnp.full((type_count, spots), -1, jnp.int32)
    for i in range(nlat):
        for p in range(positions):
            want = jnp.where(cols_i == i * positions + p, types[p, i], want)
    by_type = (lax.broadcasted_iota(jnp.int32, (type_count, spots), 0) == want).astype(F32).astype(BF16)
    ends = [t_val[pl.ds(r * beats + head_count, spots, stride=span_b), :] for r in range(per)]
    for h in range(head_count):
        pieces = []
        for r in range(per):
            pieces.append(t_val[pl.ds(r * beats + h, spots, stride=span_b), :])
            pieces.append(ends[r][:, h * spare : (h + 1) * spare])
        flat = jnp.concatenate(pieces, axis=1).astype(BF16)
        t_out[h] = jnp.dot(by_type, flat, preferred_element_type=F32)
    def total_p(i, half):
        total = lines[i][half].astype(F32)
        for j in range(1, rows_n):
            total = total + lines[i][2 * j + half].astype(F32)
        return total * scale

    for i in (0, 1):
        for j in range(1, nlat):
            line_p(i, j).wait_recv()
    sums = [total_p(0, half) for half in range(2)]
    up_o[...] = jnp.concatenate([unpack(part[top:]) for part in sums], axis=0).T
    block_qp = jnp.concatenate([unpack(part[:packed_qp]) for part in sums], axis=0)
    qkv_o[...] = block_qp[:n_qkv]
    proj_o[...] = block_qp[n_qkv:]
    gain_o[...] = sums[0][packed_qp : packed_qp + 2, :lanes]
    for half in range(2):
        down_o[:, half * wide : (half + 1) * wide] = total_p(1, half)
    for copy in outs:
        copy.wait()
    for i in range(3):
        for k in range(reach):
            if k:
                far_w(i, k).wait_send()
                pair_w(i, k, lon).wait_send()
            near_w(i, k, lon).wait_send()
            pair_w(i, reach + k, lon).wait_send()
    for i in (0, 1):
        for k in range(reach):
            if k:
                far_p(i, k).wait_send()
            near_p(i, k).wait_send()
        for j in range(1, nlat):
            line_p(i, j).wait_send()
    for g in range(3):
        for i in range(3):
            halo(g, i).wait_send()
    for p in range(positions):
        for k in range(reach):
            if k:
                far_b(p, k).wait_send()
                far_t(p, k).wait_send()
            near_b(p, k).wait_send()
            near_t(p, k).wait_send()
        for j in range(1, nlat):
            row_t(p, j).wait_send()


def shards_fused(inputs, cotangent, qkv_weight, proj_weight, up_weight, down_weight, norm_gains, bias_table, type_of, region):
    levels, rows, cols, features = inputs.shape
    nlat, nlon = lax.axis_size("lat"), lax.axis_size("lon")
    level_windows = levels // WPL
    type_count, head_count, part = bias_table.shape
    positions, owners, reach, rows_n = level_windows, nlon, nlon // 2, nlat // 2
    n_up, n_qkv, n_proj = up_weight.shape[1], qkv_weight.shape[1], proj_weight.shape[1]
    gain_cols = norm_gains.shape[1]
    height = (n_qkv + n_proj + n_up) * 3 // 4 + SUB
    down, dw = down_weight.shape[1], down_weight.shape[0] // 2
    dma = pltpu.SemaphoreType.DMA
    vmem, hbm = pl.BlockSpec(memory_space=pltpu.VMEM), pl.BlockSpec(memory_space=pltpu.HBM)
    smem = pl.BlockSpec(memory_space=pltpu.SMEM)
    cell = (rows, cols, levels, features)
    per = WIN // owners
    blk = (-(-per * (head_count + 1) // 16) * 16, LANES)
    wide = (head_count + 1) * LANES
    a_shape, d_shape = (height, LANES), (down, dw)
    sizes = [(owners * n, features) for n in (n_qkv, n_proj, n_up)] + [(features, 2 * dw)]
    v = pltpu.VMEM
    lane_tiles = -(-features // LANES)
    scratch = [v((n_qkv, features), BF16), v((n_proj, features), BF16), v((features, n_up), BF16)]
    scratch += [v((down, 2 * dw), BF16), v((2, gain_cols), BF16), v((head_count, type_count, part), BF16)]
    slim = (rows, cols, levels, LANES)
    scratch += [v((2,) + cell, BF16), v(slim, BF16), v((3,) + slim, BF16), v((owners, 2) + a_shape, BF16), v((owners, 2) + d_shape, BF16),
                v((positions, owners) + blk, BF16)]
    scratch += [v((lane_tiles, rows * cols * levels, LANES), F32)] + [v((positions, WIN, features), F32)] * 3
    scratch += [v((lane_tiles, WIN, LANES), F32), v((owners * blk[0], LANES), F32)]
    scratch += [v((head_count + 1, WIN, LANES), F32)]
    scratch += [v((WIN, wide), BF16)] * 2 + [v((wide, features), BF16)] * 2
    scratch += [v((per * SUB, LANES), F32)] * 2 + [v((positions,) + blk, F32)]
    scratch += [v(size, BF16) for size in sizes] + [v((2, features), F32)]
    scratch += [v(size, F32) for size in sizes] + [v((2, features), F32)]
    scratch += [v((2, owners) + a_shape, BF16), v((2, owners) + d_shape, BF16), v(cell, BF16)]
    scratch += [v((owners,) + s, BF16) for s in (a_shape, d_shape)] * 2
    scratch += [v((reach,) + s, BF16) for s in (a_shape, d_shape)] * 3
    scratch += [v((nlat,) + s, BF16) for s in (a_shape, d_shape)]
    scratch += [v((positions, owners) + blk, BF16)] + [v((positions, reach) + blk, BF16)] * 3
    scratch += [v((nlat, positions) + blk, BF16), v((nlat * positions * blk[0], LANES), F32)]
    scratch += [dma((6,)), dma((2,))] + [dma((3, 3))] * 2 + [dma((3, reach))] * 4 + [dma((3, nlon))] * 2
    scratch += [dma((positions, reach))] * 8 + [dma((positions, nlat))] * 2
    scratch += [dma((2,))] * 2 + [dma((2, reach))] * 4 + [dma((2, nlat))] * 2 + [dma((3,))] * 2
    outs = [(cell, BF16), ((n_qkv, features), F32), ((n_proj, features), F32), ((features, n_up), F32),
            ((down, 2 * dw), F32), ((2, gain_cols), F32), ((head_count, type_count, part), F32)]
    outs = [jax.ShapeDtypeStruct(*o) for o in outs]
    token_count = levels * rows * cols * nlat * nlon
    found = pl.pallas_call(
        functools.partial(fused_kernel, nlat, nlon, (n_up, n_qkv, n_proj), 1.0 / math.sqrt(token_count)),
        out_shape=outs,
        in_specs=[hbm] * 8 + [smem] * 2,
        out_specs=[vmem] * len(outs),
        scratch_shapes=scratch,
        compiler_params=pltpu.CompilerParams(
            collective_id=0, has_side_effects=True, vmem_limit_bytes=60 * 2**20
        ),
    )(
        inputs.transpose(1, 2, 0, 3), cotangent.transpose(1, 2, 0, 3),
        qkv_weight.T, proj_weight.T, up_weight, down_weight.T, norm_gains,
        bias_table.transpose(1, 0, 2), type_of, region,
    )
    grad, qkv, proj, up, down_g, gain, table = pl.pallas_call(
        finish_kernel,
        out_shape=outs,
        in_specs=[hbm] * len(outs),
        out_specs=[hbm] * len(outs),
        scratch_shapes=[v(o.shape, o.dtype) for o in outs] + [dma((2, len(outs)))],
        compiler_params=pltpu.CompilerParams(vmem_limit_bytes=60 * 2**20),
    )(*found)
    return grad.transpose(2, 0, 1, 3), qkv.T, proj.T, up, down_g.T, gain, table.transpose(1, 0, 2)


def shards(*args):
    inputs, bias_table = args[0], args[7]
    nlat, nlon = lax.axis_size("lat"), lax.axis_size("lon")
    levels, rows, cols, _ = inputs.shape
    heads = bias_table.shape[1]
    whole_rows = bias_table.shape[2] * nlon == WIN * WIN and nlon == SUB and WIN % nlon == 0
    one_window = rows == WLAT and cols == WLON and levels == SUB and nlat % 2 == 0
    ends_fit = WIN > LANES and (WIN - LANES) * heads <= LANES and heads < SUB
    n_qkv, n_proj, n_up, down = (args[i].shape[1] for i in (2, 3, 4, 5))
    tiled = n_qkv % SUB == 0 and (n_qkv + n_proj) % 32 == 0 and n_up % 32 == 0 and down % SUB == 0
    tiled = tiled and 2 * (inputs.shape[3] - LANES) == LANES
    if whole_rows and one_window and ends_fit and tiled:
        return shards_fused(*args)
    return shards_plain(*args)


def solution(mesh):
    return jax.shard_map(
        shards,
        mesh=mesh,
        in_specs=(
            P(None, "lat", "lon", None),
            P(None, "lat", "lon", None),
            P(None, "lon"),
            P(None, "lon"),
            P(None, "lon"),
            P(None, "lon"),
            P(None, "lon"),
            P(None, None, "lon"),
            P(),
            P(None, "lat"),
        ),
        out_specs=(
            P(None, "lat", "lon", None),
            P(None, "lon"),
            P(None, "lon"),
            P(None, "lon"),
            P(None, "lon"),
            P(None, "lon"),
            P(None, None, "lon"),
        ),
        check_vma=False,
    )
```
